32 devices in a mesh: rep: 16 (over z, y, x), shard: 2 (over core).
Axes of the slice: x: 2, y: 2, z: 4, core: 2. Of those that a mesh axis runs over, the one named last changes fastest.
Arguments:
- grad_parts: float32 [16, 2, 2, 1024, 512], P('rep', 'shard'), may hold values from -6 to 6
- weights: bfloat16 [2, 1024, 512], P(None, 'shard'), may hold values from -3 to 3
- stat_left: float32 [2, 1024, 1024], P(None, 'shard'), may hold values from -12 to 332, as said below
- stat_right: float32 [512, 512], replicated, may hold values from -12 to 238.27417, as said below
- basis_left: bfloat16 [2, 1024, 1024], P(None, 'shard'), may hold values from -0.1875 to 0.1875
- basis_right: bfloat16 [512, 512], replicated, may hold values from -0.25 to 0.25
- moment_first: float32 [2, 1024, 512], P(None, 'shard'), may hold values from -2 to 2
- moment_second: float32 [2, 1024, 512], P(None, 'shard'), may hold values from 0.05 to 1
Outputs:
- weights_new: bfloat16 [2, 1024, 512], replicated
- basis_left_new: bfloat16 [2, 1024, 1024], P(None, 'shard')
- basis_right_new: bfloat16 [512, 512], replicated
- moment_first_new: float32 [2, 1024, 512], P(None, 'shard')
- moment_second_new: float32 [2, 1024, 512], P(None, 'shard')
The draws below stay inside these ranges and needn't reach their ends.
Inputs may be any that keep to these rules, and one draw needn't show every extreme that they name: `stat_left`: each block is a symmetric matrix. `stat_right`: a symmetric matrix.
All inputs are finite; a program needn't handle non-finite values.
Results may differ from the reference program's by a relative error of at most 0.015.
Values may be sent and summed in bfloat16 or wider, within the bound.
A program may use at most 128 MiB of HBM per device.

```python
import math
import jax
import jax.numpy as jnp
from jax import lax

D = 2048
KV = 512
BLK = 1024
NS_ITERS = 3
NBLK = 2
N_REP = 16
N_SHARD = 2


def symmetric_stat(key, block_count, block_size):
    key_noise = jax.random.fold_in(key, 11)
    key_diagonal = jax.random.fold_in(key, 12)
    noise_values = jnp.clip(jax.random.normal(key_noise, (block_count, block_size, block_size), jnp.float32), -3.0, 3.0)
    symmetric = 0.5 * (noise_values + jnp.swapaxes(noise_values, 1, 2))
    diagonal = jnp.exp(jax.random.uniform(key_diagonal, (block_count, block_size), jnp.float32, 0.0, math.log(10.0))) * math.sqrt(block_size)
    identity = (jnp.arange(block_size)[:, None] == jnp.arange(block_size)[None, :]).astype(jnp.float32)
    return symmetric + identity[None, :, :] * diagonal[:, :, None]


def draw_stat_left(key, part):
    return symmetric_stat(key, D // BLK, BLK)


def draw_stat_right(key, part):
    return symmetric_stat(key, 1, KV).reshape(KV, KV)


def spiked(result, rng, source, target, parts, factor):
    def block_of(position):
        return (jnp.arange(result.shape[position]) // (result.shape[position] // parts)).reshape((-1,) + (1,) * (result.ndim - 1 - position))

    first = jax.random.permutation(rng, parts)[block_of(target)]
    far = (block_of(target) + parts // 2) % parts
    return jnp.where((block_of(source) == first) | (block_of(source) == far), factor * result, result)


def shard_levels(rng, shape, shards, low, high):
    factor_of = 1.0
    for axis_at, blocks in shards:
        steps = jax.random.uniform(jax.random.fold_in(jax.random.fold_in(rng, 6), axis_at), (blocks,), jnp.float32, low / len(shards), high / len(shards))
        factor_of = factor_of * jnp.repeat(jnp.exp(steps), shape[axis_at] // blocks).reshape((-1,) + (1,) * (len(shape) - 1 - axis_at))
    return factor_of


def gaussian(own_key, dims, scale, bound, pieces=(), dtype=jnp.bfloat16):
    gain = shard_levels(own_key, dims, pieces, -0.22, 0.18) if pieces else 1.0
    result = jax.random.normal(own_key, dims, jnp.float32) * scale * gain
    return jnp.minimum(jnp.maximum(result, -bound), bound).astype(dtype)


def bell_draw_with(key, extent, width, bound, pieces, heavy, dtype=jnp.bfloat16):
    drawn = width * jax.random.normal(key, extent, jnp.float32)
    if pieces:
        drawn = drawn * shard_levels(key, extent, pieces, -0.22, 0.18)
    return jnp.clip(spiked(drawn, jax.random.fold_in(key, 3), *heavy), -bound, bound).astype(dtype)


def setup_inputs(seed: int = 0) -> dict:
    keys = jax.random.split(jax.random.key(seed), 9)
    return {
        "grad_parts": bell_draw_with(keys[0], (N_REP, N_SHARD, NBLK, BLK, KV), 1.0, 6.0, ((0, 16), (1, 2)), (1, 3, 2, 2.0), jnp.float32),
        "weights": gaussian(keys[1], (NBLK, BLK, KV), 0.5, 3.0, ((1, 2),)),
        "stat_left": draw_stat_left(jax.random.fold_in(keys[8], 71), 0),
        "stat_right": draw_stat_right(jax.random.fold_in(keys[8], 71), 0),
        "basis_left": gaussian(keys[4], (NBLK, BLK, BLK), BLK ** -0.5, 0.1875, ((1, 2),)),
        "basis_right": gaussian(keys[5], (KV, KV), KV ** -0.5, 0.25),
        "moment_first": gaussian(keys[6], (NBLK, BLK, KV), 0.3, 2.0, ((1, 2),), jnp.float32),
        "moment_second": jnp.clip(jnp.exp(math.log(1.0) - 2.9957323 * jax.random.uniform(keys[7], (NBLK, BLK, KV), jnp.float32) ** shard_levels(keys[7], (NBLK, BLK, KV), ((1, 2),), -0.2, 0.2)), 0.05, 1.0),
    }


stat_beta = 0.9
moment_decay = 0.9
square_decay = 0.95
learn_rate = 0.1
epsilon = 1e-08
norm_epsilon = 1e-06
schulz_linear = 3.4445
schulz_cubic = -4.775
schulz_quintic = 2.0315

def schulz(matrix):
    current = matrix
    for sweep_index in range(NS_ITERS):
        gram_matrix = lax.optimization_barrier(jnp.dot(current, current.T, preferred_element_type=jnp.float32).astype(jnp.bfloat16))
        poly_matrix = (schulz_cubic * gram_matrix.astype(jnp.float32) + schulz_quintic * jnp.dot(gram_matrix, gram_matrix, preferred_element_type=jnp.float32)).astype(jnp.bfloat16)
        current = (schulz_linear * current.astype(jnp.float32) + jnp.dot(poly_matrix, current, preferred_element_type=jnp.float32)).astype(jnp.bfloat16)
    return current

def power_start(statistic, basis_old):
    power_rows = jnp.dot(statistic.astype(jnp.bfloat16), basis_old, preferred_element_type=jnp.float32)
    return (power_rows * lax.rsqrt(jnp.sum(power_rows * power_rows) + norm_epsilon)).astype(jnp.bfloat16)

def reference(grad_parts, weights, stat_left, stat_right, basis_left, basis_right, moment_first, moment_second):
    grad_mean = lax.optimization_barrier(jnp.sum(grad_parts, axis=(0, 1))) / N_REP
    grad_low = grad_mean.astype(jnp.bfloat16)
    grad_flat = grad_low.reshape(D, KV)
    right_new = stat_beta * stat_right + (1.0 - stat_beta) * jnp.dot(grad_flat.T, grad_flat, preferred_element_type=jnp.float32)
    basis_right_new = schulz(power_start(right_new, basis_right))
    left_blocks = []
    rotate_blocks = []
    for block_index in range(D // BLK):
        grad_block = grad_low[block_index]
        left_new = stat_beta * stat_left[block_index] + (1.0 - stat_beta) * jnp.dot(grad_block, grad_block.T, preferred_element_type=jnp.float32)
        left_blocks.append(schulz(power_start(left_new, basis_left[block_index])))
        rotate_blocks.append(jnp.dot(basis_left[block_index].T, grad_block, preferred_element_type=jnp.float32))
    rot_left = jnp.stack(rotate_blocks, 0)
    rotated = jnp.dot(rot_left.reshape(D, KV).astype(jnp.bfloat16), basis_right, preferred_element_type=jnp.float32).reshape(D // BLK, BLK, KV)
    moment_new = moment_decay * moment_first + (1.0 - moment_decay) * rotated
    square_new = square_decay * moment_second + (1.0 - square_decay) * rotated * rotated
    direction = moment_new / (jnp.sqrt(square_new) + epsilon)
    half_turn = jnp.dot(direction.reshape(D, KV).astype(jnp.bfloat16), basis_right.T, preferred_element_type=jnp.float32).astype(jnp.bfloat16).reshape(D // BLK, BLK, KV)
    update_blocks = []
    for block_index in range(D // BLK):
        update_blocks.append(jnp.dot(basis_left[block_index], half_turn[block_index], preferred_element_type=jnp.float32))
    update = jnp.stack(update_blocks, 0)
    weights_new = (weights.astype(jnp.float32) - learn_rate * update).astype(jnp.bfloat16)
    return (weights_new, jnp.stack(left_blocks, 0), basis_right_new, moment_new, square_new)
```

```python
import functools

import jax
import jax.numpy as jnp
from jax import lax
from jax.experimental import pallas as pl
from jax.experimental.pallas import tpu as pltpu
from jax.sharding import PartitionSpec as P

NS_ITERS = 3


stat_beta = 0.9
moment_decay = 0.9
square_decay = 0.95
learn_rate = 0.1
epsilon = 1e-08
norm_epsilon = 1e-06
schulz_linear = 3.4445
schulz_cubic = -4.775
schulz_quintic = 2.0315


def schulz_whole(matrix):
    current = matrix
    for sweep_index in range(NS_ITERS):
        gram_matrix = lax.optimization_barrier(
            jnp.dot(current, current.T, preferred_element_type=jnp.float32).astype(jnp.bfloat16)
        )
        poly_matrix = (
            schulz_cubic * gram_matrix.astype(jnp.float32)
            + schulz_quintic * jnp.dot(gram_matrix, gram_matrix, preferred_element_type=jnp.float32)
        ).astype(jnp.bfloat16)
        current = (
            schulz_linear * current.astype(jnp.float32)
            + jnp.dot(poly_matrix, current, preferred_element_type=jnp.float32)
        ).astype(jnp.bfloat16)
    return current


def schulz_split(start_rows):
    current = start_rows
    for sweep_index in range(NS_ITERS):
        gathered = lax.all_gather(current, "shard", axis=1, tiled=True)
        gram_rows = lax.optimization_barrier(
            jnp.einsum(
                "bik,bjk->bij", current, gathered, preferred_element_type=jnp.float32
            ).astype(jnp.bfloat16)
        )
        gram_block = lax.all_gather(gram_rows, "shard", axis=1, tiled=True)
        poly_rows = (
            schulz_cubic * gram_rows.astype(jnp.float32)
            + schulz_quintic
            * jnp.einsum("bij,bjk->bik", gram_rows, gram_block, preferred_element_type=jnp.float32)
        ).astype(jnp.bfloat16)
        current = (
            schulz_linear * current.astype(jnp.float32)
            + jnp.einsum("bij,bjk->bik", poly_rows, gathered, preferred_element_type=jnp.float32)
        ).astype(jnp.bfloat16)
    return current


def on_device(
    grad_parts, weights, stat_left, stat_right, basis_left, basis_right, moment_first, moment_second
):
    block_count = weights.shape[0]
    row_count = weights.shape[1]
    width_kv = weights.shape[2]
    rep_count = lax.axis_size("rep")
    shard_pos = lax.axis_index("shard")
    row_start = shard_pos * row_count
    partial_value = grad_parts[0, 0]
    grad_total = lax.psum(partial_value, ("rep", "shard")) / rep_count
    grad_full = grad_total.astype(jnp.bfloat16)
    grad_rows = lax.dynamic_slice_in_dim(grad_full, row_start, row_count, 1)
    left_new = stat_beta * stat_left + (1.0 - stat_beta) * jnp.einsum(
        "bik,bjk->bij", grad_rows, grad_full, preferred_element_type=jnp.float32
    )
    grad_flat = grad_rows.reshape(block_count * row_count, width_kv)
    right_terms = jnp.dot(grad_flat.T, grad_flat, preferred_element_type=jnp.float32)
    right_new = stat_beta * stat_right + (1.0 - stat_beta) * lax.psum(right_terms, "shard")
    basis_all = lax.all_gather(basis_left, "shard", axis=1, tiled=True)
    power_rows = jnp.einsum(
        "bij,bjk->bik", left_new.astype(jnp.bfloat16), basis_all, preferred_element_type=jnp.float32
    )
    local_squares = jnp.sum(power_rows * power_rows, axis=(1, 2))
    block_squares = lax.psum(local_squares, "shard")
    start_rows = (power_rows * lax.rsqrt(block_squares + norm_epsilon)[:, None, None]).astype(
        jnp.bfloat16
    )
    basis_left_new = schulz_split(start_rows)
    right_power = jnp.dot(
        right_new.astype(jnp.bfloat16), basis_right, preferred_element_type=jnp.float32
    )
    right_start = (
        right_power * lax.rsqrt(jnp.sum(right_power * right_power) + norm_epsilon)
    ).astype(jnp.bfloat16)
    basis_right_new = schulz_whole(right_start)
    local_turn = jnp.einsum(
        "bji,bjk->bik", basis_left, grad_rows, preferred_element_type=jnp.float32
    )
    rot_left = lax.psum_scatter(
        local_turn.astype(jnp.bfloat16), "shard", scatter_dimension=1, tiled=True
    ).astype(jnp.float32)
    rot_flat = rot_left.reshape(block_count * row_count, width_kv).astype(jnp.bfloat16)
    rotated = jnp.dot(rot_flat, basis_right, preferred_element_type=jnp.float32).reshape(
        block_count, row_count, width_kv
    )
    moment_new = moment_decay * moment_first + (1.0 - moment_decay) * rotated
    square_new = square_decay * moment_second + (1.0 - square_decay) * rotated * rotated
    direction = moment_new / (jnp.sqrt(square_new) + epsilon)
    direction_flat = direction.reshape(block_count * row_count, width_kv).astype(jnp.bfloat16)
    half_turn = (
        jnp.dot(direction_flat, basis_right.T, preferred_element_type=jnp.float32)
        .astype(jnp.bfloat16)
        .reshape(block_count, row_count, width_kv)
    )
    half_all = lax.all_gather(half_turn, "shard", axis=1, tiled=True)
    update = jnp.einsum("bij,bjk->bik", basis_left, half_all, preferred_element_type=jnp.float32)
    weight_rows_new = (weights.astype(jnp.float32) - learn_rate * update).astype(jnp.bfloat16)
    weights_new = lax.all_gather(weight_rows_new, "shard", axis=1, tiled=True)
    return (weights_new, basis_left_new, basis_right_new, moment_new, square_new)


MESH = pl.DeviceIdType.MESH
PLANE = 4
LINE = 4
ORDER = (2, 1, 3, 0)
F32 = jnp.float32
BF16 = jnp.bfloat16


def dot(a, b, dims=((1,), (0,))):
    return lax.dot_general(a, b, (dims, ((), ())), preferred_element_type=F32)


def tile_rows(at, tile):
    return pl.ds(pl.multiple_of(at * tile, tile), tile)


def schulz_sweeps(start, gram, spare, size, tile):
    chain = (start, spare, start, spare)
    for sweep in range(NS_ITERS):
        now, later = chain[sweep % 2], chain[sweep % 2 + 1]

        @pl.loop(0, size // tile)
        def _(at):
            rows = tile_rows(at, tile)
            gram[rows, :] = dot(now[rows, :], now[...], ((1,), (1,))).astype(BF16)

        @pl.loop(0, size // tile)
        def _(at):
            rows = tile_rows(at, tile)
            poly = schulz_cubic * gram[rows, :].astype(F32) + schulz_quintic * dot(gram[rows, :], gram[...])
            later[rows, :] = (
                schulz_linear * now[rows, :].astype(F32) + dot(poly.astype(BF16), now[...])
            ).astype(BF16)
    return later


def step_kernel(
    parts, weights_in, stat_in, stat_right, basis_in, right, first_in, second_in,
    weights_out, basis_out, right_out, first_out, second_out,
    far_part, near_part, pair_send, pair_recv, chip_low, plane_recv, line_send, line_recv,
    grad, basis, stat, first, second, weights,
    power, rot, rot_sum, half, start, spare, gram, rpower, rterm,
    load_sem, pair_sem, plane_sem, line_sem, gline_sem, gplane_sem, gpair_sem, swap_sem, keep_sem,
    give_sem, store_sem,
):
    rep = lax.axis_index("rep")
    core = lax.axis_index("shard")
    other = 1 - core
    layer = rep // PLANE
    spot = lax.rem(rep, PLANE)
    size = basis.shape[0]
    height = basis_in.shape[1]
    piece = size // (PLANE * LINE)
    tile = 256

    def line_of(k):
        return lax.rem(layer + k, LINE)

    def spot_of(j):
        return lax.rem(spot + j, PLANE)

    def rows_of(p, z):
        return pl.ds(pl.multiple_of((z * PLANE + p) * piece, piece), piece)

    loads = {}
    for k in ORDER:
        far = pltpu.make_async_copy(parts.at[other, line_of(k)], far_part.at[k], load_sem.at[0, k])
        far.start()
        near = pltpu.make_async_copy(parts.at[core, line_of(k)], near_part.at[k], load_sem.at[1, k])
        near.start()
        loads[k] = (far, near)
    mine = pl.ds(pl.multiple_of(core * height, height), height)
    theirs = pl.ds(pl.multiple_of(other * height, height), height)
    moved = ((stat_in, stat), (basis_in, basis), (first_in, first), (second_in, second), (weights_in, weights))
    keeps = []
    for at, (source, target) in enumerate(moved):
        keep = pltpu.make_async_copy(source.at[core], target.at[mine], keep_sem.at[at])
        keep.start()
        keeps.append(keep)

    barrier = pltpu.get_barrier_semaphore()
    partners = [(rep, other)]
    partners += [(layer * PLANE + spot_of(j), core) for j in range(1, PLANE)]
    partners += [(line_of(k) * PLANE + spot, core) for k in range(1, LINE)]
    for partner in partners:
        pl.semaphore_signal(barrier, inc=1, device_id=partner, device_id_type=MESH)
    pl.semaphore_wait(barrier, len(partners))

    def send(source, target, sems, partner):
        copy = pltpu.make_async_remote_copy(
            src_ref=source, dst_ref=target, send_sem=sems.at[0], recv_sem=sems.at[1],
            device_id=partner, device_id_type=MESH,
        )
        copy.start()
        return copy

    pairs = {}
    for k in ORDER:
        loads[k][0].wait()
        pair_send[k] = far_part[k].astype(BF16)
        pairs[k] = send(pair_send.at[k], pair_recv.at[k], pair_sem.at[k], (rep, other))

    planes = {}
    for k in ORDER:
        loads[k][1].wait()
        pairs[k].wait_recv()
        near_part[k] = near_part[k] + pair_recv[k].astype(F32)
        chip_low[k] = near_part[k].astype(BF16)
        for j in (2, 1, 3):
            planes[k, j] = send(
                chip_low.at[k, spot_of(j)], plane_recv.at[k, j - 1], plane_sem.at[k, j - 1],
                (layer * PLANE + spot_of(j), core),
            )

    swaps = []
    for at, (source, target) in enumerate(moved):
        swaps.append(send(source.at[other], target.at[mine], swap_sem.at[at], (rep, other)))

    lines = {}
    total = None
    for k in ORDER:
        for j in range(1, PLANE):
            planes[k, j].wait_recv()
        total = near_part[k, spot]
        for j in range(1, PLANE):
            total = total + plane_recv[k, j - 1].astype(F32)
        if k:
            line_send[k - 1] = total.astype(BF16)
            lines[k] = send(
                line_send.at[k - 1], line_recv.at[k - 1], line_sem.at[k - 1],
                (line_of(k) * PLANE + spot, core),
            )
    for k in range(1, LINE):
        lines[k].wait_recv()
        total = total + line_recv[k - 1].astype(F32)
    own = rows_of(spot, layer)
    grad[core, own, :] = (total * (1.0 / (PLANE * LINE))).astype(BF16)

    def share(rows, sems, partner):
        return send(grad.at[core, rows], grad.at[core, rows], sems, partner)

    glines = {k: share(own, gline_sem.at[k - 1], (line_of(k) * PLANE + spot, core)) for k in (2, 1, 3)}
    gplanes = {}
    gpairs = []
    for at, k in enumerate((0, 1, 3, 2)):
        rows = rows_of(spot, lax.rem(layer + LINE - k, LINE))
        if k:
            glines[k].wait_recv()
        for j in (2, 1, 3):
            gplanes[k, j] = share(rows, gplane_sem.at[k, j - 1], (layer * PLANE + spot_of(j), core))
        gpairs.append(share(rows, gpair_sem.at[k, 0], (rep, other)))
        if at == 0:
            for step in (0, 1):
                swaps[step].wait_recv()
                keeps[step].wait()
        rows = pl.ds(at * (size // LINE), size // LINE)
        power[rows, :] = stat_beta * dot(stat[rows, :].astype(BF16), basis[...])
    for k in (0, 1, 3, 2):
        for j in (1, 3, 2):
            gplanes[k, j].wait_recv()
            rows = rows_of(lax.rem(spot + PLANE - j, PLANE), lax.rem(layer + LINE - k, LINE))
            gpairs.append(share(rows, gpair_sem.at[k, j], (rep, other)))
        group = tile_rows(lax.rem(layer + LINE - k, LINE), size // LINE)
        if k == 0:
            rterm[...] = dot(grad[core, group, :], grad[core, group, :], ((0,), (0,)))
        else:
            rterm[...] += dot(grad[core, group, :], grad[core, group, :], ((0,), (0,)))

        @pl.loop(0, size // tile)
        def _(at):
            rows = tile_rows(at, tile)
            added = dot(basis[group, rows], grad[core, group, :], ((0,), (0,)))
            if k == 0:
                rot_sum[rows, :] = added
            else:
                rot_sum[rows, :] += added
    for step in (2, 3, 4):
        swaps[step].wait_recv()
        keeps[step].wait()

    @pl.loop(0, size // tile)
    def _(at):
        rows = tile_rows(at, tile)
        turned = rot_sum[rows, :].astype(BF16)
        rot[rows, :] = turned
        rotated = dot(turned, right[...])
        moment = moment_decay * first[rows, :] + (1.0 - moment_decay) * rotated
        square = square_decay * second[rows, :] + (1.0 - square_decay) * rotated * rotated
        first[rows, :] = moment
        second[rows, :] = square
        direction = moment / (jnp.sqrt(square) + epsilon)
        half[rows, :] = dot(direction.astype(BF16), right[...], ((1,), (1,))).astype(BF16)

    @pl.loop(0, size // tile)
    def _(at):
        rows = tile_rows(at, tile)
        update = dot(basis[rows, :], half[...])
        weights[rows, :] = (weights[rows, :].astype(F32) - learn_rate * update).astype(BF16)

    gives = []
    stores = []

    def store(source, target):
        copy = pltpu.make_async_copy(source, target, store_sem.at[len(stores)])
        copy.start()
        stores.append(copy)

    def give(source, target):
        gives.append(send(source, target, give_sem.at[len(gives)], (rep, other)))

    give(weights, weights_out.at[core])
    give(first.at[theirs], first_out.at[core])
    give(second.at[theirs], second_out.at[core])
    store(weights, weights_out.at[core])
    store(first.at[mine], first_out.at[core])
    store(second.at[mine], second_out.at[core])

    def left_tile(at, squares):
        rows = tile_rows(at, tile)
        value = power[rows, :] + (1.0 - stat_beta) * dot(grad[core, rows, :], rot[...], ((1,), (1,)))
        power[rows, :] = value
        return squares + jnp.sum(value * value)

    squares = lax.fori_loop(0, size // tile, left_tile, jnp.float32(0.0))
    scale = lax.rsqrt(squares + norm_epsilon)

    @pl.loop(0, size // tile)
    def _(at):
        rows = tile_rows(at, tile)
        start[rows, :] = (power[rows, :] * scale).astype(BF16)

    left = schulz_sweeps(start, gram, spare, size, size)
    give(left.at[theirs], basis_out.at[core])
    store(left.at[mine], basis_out.at[core])

    for copy in gpairs:
        copy.wait_recv()
    width = right.shape[0]

    def right_tile(at, squares):
        rows = tile_rows(at, tile)
        terms = rterm[rows, :] + dot(grad[other, :, rows], grad[other], ((0,), (0,)))
        mixed = stat_beta * stat_right[rows, :] + (1.0 - stat_beta) * terms
        value = dot(mixed.astype(BF16), right[...])
        rpower[rows, :] = value
        return squares + jnp.sum(value * value)

    rsquares = lax.fori_loop(0, width // tile, right_tile, jnp.float32(0.0))
    rscale = lax.rsqrt(rsquares + norm_epsilon)
    right_out[...] = (rpower[...] * rscale).astype(BF16)

    for copy in gives:
        copy.wait_recv()
    for group in (pairs, planes, lines, glines, gplanes):
        for copy in group.values():
            copy.wait_send()
    for copy in gpairs + swaps + gives:
        copy.wait_send()
    for copy in stores:
        copy.wait()


def finish_kernel(
    start, weights, basis, first, second, right_out, weights_out, basis_out, first_out, second_out,
    now, spare, gram, store_sem,
):
    moves = ((weights, weights_out), (basis, basis_out), (first, first_out), (second, second_out))
    stores = []
    for at, (source, target) in enumerate(moves):
        store = pltpu.make_async_copy(source, target, store_sem.at[at])
        store.start()
        stores.append(store)
    now[...] = start[...]
    right_out[...] = schulz_sweeps(now, gram, spare, now.shape[0], now.shape[0])[...]
    for store in stores:
        store.wait()


def finish_right(start, *held):
    anywhere = pl.BlockSpec(memory_space=pl.ANY)
    in_vmem = pl.BlockSpec(memory_space=pltpu.VMEM)
    width = start.shape[0]
    return pl.pallas_call(
        finish_kernel,
        out_shape=[jax.ShapeDtypeStruct(a.shape, a.dtype) for a in (start,) + held],
        in_specs=[in_vmem] * 5,
        out_specs=[in_vmem] + [anywhere] * 4,
        scratch_shapes=[pltpu.VMEM((width, width), BF16)] * 3 + [pltpu.SemaphoreType.DMA((4,))],
        compiler_params=pltpu.CompilerParams(vmem_limit_bytes=8 << 20),
    )(start, *held)


def on_device_blocks(
    grad_parts, weights, stat_left, stat_right, basis_left, basis_right, moment_first, moment_second
):
    blocks, height, width = weights.shape
    size = blocks * height
    piece = size // (PLANE * LINE)
    parts = grad_parts.reshape(blocks, LINE, PLANE, piece, width)
    anywhere = pl.BlockSpec(memory_space=pl.ANY)
    in_vmem = pl.BlockSpec(memory_space=pltpu.VMEM)
    dma = pltpu.SemaphoreType.DMA
    weights_new, left_new, right_start, first_new, second_new = pl.pallas_call(
        step_kernel,
        out_shape=(
            pltpu.VMEM((blocks, size, width), BF16),
            pltpu.VMEM((blocks, height, size), BF16),
            pltpu.VMEM((width, width), BF16),
            pltpu.VMEM((blocks, height, width), F32),
            pltpu.VMEM((blocks, height, width), F32),
        ),
        in_specs=[anywhere, anywhere, anywhere, in_vmem, anywhere, in_vmem, anywhere, anywhere],
        out_specs=(in_vmem,) * 5,
        scratch_shapes=[
            pltpu.VMEM((LINE, PLANE, piece, width), F32),
            pltpu.VMEM((LINE, PLANE, piece, width), F32),
            pltpu.VMEM((LINE, PLANE, piece, width), BF16),
            pltpu.VMEM((LINE, PLANE, piece, width), BF16),
            pltpu.VMEM((LINE, PLANE, piece, width), BF16),
            pltpu.VMEM((LINE, PLANE - 1, piece, width), BF16),
            pltpu.VMEM((LINE - 1, piece, width), BF16),
            pltpu.VMEM((LINE - 1, piece, width), BF16),
            pltpu.VMEM((blocks, size, width), BF16),
            pltpu.VMEM((size, size), BF16),
            pltpu.VMEM((size, size), F32),
            pltpu.VMEM((size, width), F32),
            pltpu.VMEM((size, width), F32),
            pltpu.VMEM((size, width), BF16),
            pltpu.VMEM((size, size), F32),
            pltpu.VMEM((size, width), BF16),
            pltpu.VMEM((size, width), F32),
            pltpu.VMEM((size, width), BF16),
            pltpu.VMEM((size, size), BF16),
            pltpu.VMEM((size, size), BF16),
            pltpu.VMEM((size, size), BF16),
            pltpu.VMEM((width, width), F32),
            pltpu.VMEM((width, width), F32),
            dma((2, LINE)),
            dma((LINE, 2)),
            dma((LINE, PLANE - 1, 2)),
            dma((LINE - 1, 2)),
            dma((LINE - 1, 2)),
            dma((LINE, PLANE - 1, 2)),
            dma((LINE, PLANE, 2)),
            dma((5, 2)),
            dma((5,)),
            dma((4, 2)),
            dma((4,)),
        ],
        compiler_params=pltpu.CompilerParams(
            collective_id=0, has_side_effects=True, vmem_limit_bytes=48 << 20
        ),
    )(parts, weights, stat_left, stat_right, basis_left, basis_right, moment_first, moment_second)
    right_new, weights_new, left_new, first_new, second_new = finish_right(
        right_start, weights_new, left_new, first_new, second_new
    )
    return weights_new, left_new, right_new, first_new, second_new


def solution(mesh):
    fits = mesh.shape["shard"] == 2 and mesh.shape["rep"] == 16
    body = on_device_blocks if fits else on_device
    placed = (
        P("rep", "shard", None, None, None),
        P(None, "shard", None),
        P(None, "shard", None),
        P(),
        P(None, "shard", None),
        P(),
        P(None, "shard", None),
        P(None, "shard", None),
    )
    return jax.shard_map(
        body,
        mesh=mesh,
        in_specs=placed,
        out_specs=(
            P(),
            P(None, "shard", None),
            P(),
            P(None, "shard", None),
            P(None, "shard", None),
        ),
        check_vma=False,
    )
```

```python
import functools

import jax
import jax.numpy as jnp
from jax import lax
from jax.experimental import pallas as pl
from jax.experimental.pallas import tpu as pltpu
from jax.sharding import PartitionSpec as P

NS_ITERS = 3


stat_beta = 0.9
moment_decay = 0.9
square_decay = 0.95
learn_rate = 0.1
epsilon = 1e-08
norm_epsilon = 1e-06
schulz_linear = 3.4445
schulz_cubic = -4.775
schulz_quintic = 2.0315


def schulz_whole(matrix):
    current = matrix
    for sweep_index in range(NS_ITERS):
        gram_matrix = lax.optimization_barrier(
            jnp.dot(current, current.T, preferred_element_type=jnp.float32).astype(jnp.bfloat16)
        )
        poly_matrix = (
            schulz_cubic * gram_matrix.astype(jnp.float32)
            + schulz_quintic * jnp.dot(gram_matrix, gram_matrix, preferred_element_type=jnp.float32)
        ).astype(jnp.bfloat16)
        current = (
            schulz_linear * current.astype(jnp.float32)
            + jnp.dot(poly_matrix, current, preferred_element_type=jnp.float32)
        ).astype(jnp.bfloat16)
    return current


def schulz_split(start_rows):
    current = start_rows
    for sweep_index in range(NS_ITERS):
        gathered = lax.all_gather(current, "shard", axis=1, tiled=True)
        gram_rows = lax.optimization_barrier(
            jnp.einsum(
                "bik,bjk->bij", current, gathered, preferred_element_type=jnp.float32
            ).astype(jnp.bfloat16)
        )
        gram_block = lax.all_gather(gram_rows, "shard", axis=1, tiled=True)
        poly_rows = (
            schulz_cubic * gram_rows.astype(jnp.float32)
            + schulz_quintic
            * jnp.einsum("bij,bjk->bik", gram_rows, gram_block, preferred_element_type=jnp.float32)
        ).astype(jnp.bfloat16)
        current = (
            schulz_linear * current.astype(jnp.float32)
            + jnp.einsum("bij,bjk->bik", poly_rows, gathered, preferred_element_type=jnp.float32)
        ).astype(jnp.bfloat16)
    return current


def on_device(
    grad_parts, weights, stat_left, stat_right, basis_left, basis_right, moment_first, moment_second
):
    block_count = weights.shape[0]
    row_count = weights.shape[1]
    width_kv = weights.shape[2]
    rep_count = lax.axis_size("rep")
    shard_pos = lax.axis_index("shard")
    row_start = shard_pos * row_count
    partial_value = grad_parts[0, 0]
    grad_total = lax.psum(partial_value, ("rep", "shard")) / rep_count
    grad_full = grad_total.astype(jnp.bfloat16)
    grad_rows = lax.dynamic_slice_in_dim(grad_full, row_start, row_count, 1)
    left_new = stat_beta * stat_left + (1.0 - stat_beta) * jnp.einsum(
        "bik,bjk->bij", grad_rows, grad_full, preferred_element_type=jnp.float32
    )
    grad_flat = grad_rows.reshape(block_count * row_count, width_kv)
    right_terms = jnp.dot(grad_flat.T, grad_flat, preferred_element_type=jnp.float32)
    right_new = stat_beta * stat_right + (1.0 - stat_beta) * lax.psum(right_terms, "shard")
    basis_all = lax.all_gather(basis_left, "shard", axis=1, tiled=True)
    power_rows = jnp.einsum(
        "bij,bjk->bik", left_new.astype(jnp.bfloat16), basis_all, preferred_element_type=jnp.float32
    )
    local_squares = jnp.sum(power_rows * power_rows, axis=(1, 2))
    block_squares = lax.psum(local_squares, "shard")
    start_rows = (power_rows * lax.rsqrt(block_squares + norm_epsilon)[:, None, None]).astype(
        jnp.bfloat16
    )
    basis_left_new = schulz_split(start_rows)
    right_power = jnp.dot(
        right_new.astype(jnp.bfloat16), basis_right, preferred_element_type=jnp.float32
    )
    right_start = (
        right_power * lax.rsqrt(jnp.sum(right_power * right_power) + norm_epsilon)
    ).astype(jnp.bfloat16)
    basis_right_new = schulz_whole(right_start)
    local_turn = jnp.einsum(
        "bji,bjk->bik", basis_left, grad_rows, preferred_element_type=jnp.float32
    )
    rot_left = lax.psum_scatter(
        local_turn.astype(jnp.bfloat16), "shard", scatter_dimension=1, tiled=True
    ).astype(jnp.float32)
    rot_flat = rot_left.reshape(block_count * row_count, width_kv).astype(jnp.bfloat16)
    rotated = jnp.dot(rot_flat, basis_right, preferred_element_type=jnp.float32).reshape(
        block_count, row_count, width_kv
    )
    moment_new = moment_decay * moment_first + (1.0 - moment_decay) * rotated
    square_new = square_decay * moment_second + (1.0 - square_decay) * rotated * rotated
    direction = moment_new / (jnp.sqrt(square_new) + epsilon)
    direction_flat = direction.reshape(block_count * row_count, width_kv).astype(jnp.bfloat16)
    half_turn = (
        jnp.dot(direction_flat, basis_right.T, preferred_element_type=jnp.float32)
        .astype(jnp.bfloat16)
        .reshape(block_count, row_count, width_kv)
    )
    half_all = lax.all_gather(half_turn, "shard", axis=1, tiled=True)
    update = jnp.einsum("bij,bjk->bik", basis_left, half_all, preferred_element_type=jnp.float32)
    weight_rows_new = (weights.astype(jnp.float32) - learn_rate * update).astype(jnp.bfloat16)
    weights_new = lax.all_gather(weight_rows_new, "shard", axis=1, tiled=True)
    return (weights_new, basis_left_new, basis_right_new, moment_new, square_new)


MESH = pl.DeviceIdType.MESH
PLANE = 4
LINE = 4
ORDER = (2, 1, 3, 0)
GATHER = (2, 1, 3)
F32 = jnp.float32
BF16 = jnp.bfloat16


def dot(a, b, dims=((1,), (0,))):
    return lax.dot_general(a, b, (dims, ((), ())), preferred_element_type=F32)


def tile_rows(at, tile):
    return pl.ds(pl.multiple_of(at * tile, tile), tile)


def schulz_sweeps(start, gram, spare, size, tile):
    chain = (start, spare, start, spare)
    for sweep in range(NS_ITERS):
        now, later = chain[sweep % 2], chain[sweep % 2 + 1]

        @pl.loop(0, size // tile)
        def _(at):
            rows = tile_rows(at, tile)
            gram[rows, :] = dot(now[rows, :], now[...], ((1,), (1,))).astype(BF16)

        @pl.loop(0, size // tile)
        def _(at):
            rows = tile_rows(at, tile)
            poly = schulz_cubic * gram[rows, :].astype(F32) + schulz_quintic * dot(gram[rows, :], gram[...])
            later[rows, :] = (
                schulz_linear * now[rows, :].astype(F32) + dot(poly.astype(BF16), now[...])
            ).astype(BF16)
    return later


def mirror_product(target, size, tile, product):
    for at in range(0, size, tile):
        low = product(slice(at, size), slice(at, at + tile)).astype(BF16)
        target[at:, at:at + tile] = low
        if at + tile < size:
            target[at:at + tile, at + tile:] = low[tile:].T


def schulz_mirrored(start, gram, poly, spare, size, tile, emit):
    chain = (start, spare, start)
    for sweep in range(NS_ITERS):
        now = chain[sweep]
        mirror_product(gram, size, tile, lambda rows, cols: dot(now[rows, :], now[cols, :], ((1,), (1,))))
        mirror_product(
            poly, size, tile,
            lambda rows, cols: schulz_cubic * gram[rows, cols].astype(F32)
            + schulz_quintic * dot(gram[rows, :], gram[:, cols]),
        )

        def sweep_rows(rows):
            return (schulz_linear * now[rows, :].astype(F32) + dot(poly[rows, :], now[...])).astype(BF16)

        if sweep + 1 < NS_ITERS:
            chain[sweep + 1][...] = sweep_rows(slice(None))
        else:
            emit(sweep_rows)


def step_kernel(
    parts, weights_in, stat_in, stat_right_in, basis_in, right_in, first_in, second_in,
    weights_out, basis_out, right_out, first_out, second_out,
    far_part, near_part, pair_send, pair_recv, one_send, one_recv, two_send, two_recv, line_send, line_recv,
    grad, basis, stat, first, second, weights,
    power, rot, rot_sum, half, start, spare, gram, poly, rpower, rterm, rterm_far, stat_right, right,
    load_sem, pair_sem, one_sem, two_sem, line_sem, gline_sem, gtwo_sem, gone_sem, rterm_sem, swap_sem, keep_sem,
    give_sem, store_sem,
):
    rep = lax.axis_index("rep")
    core = lax.axis_index("shard")
    other = 1 - core
    layer = rep // PLANE
    y = lax.rem(rep // 2, 2)
    x = lax.rem(rep, 2)
    size = basis.shape[0]
    height = basis_in.shape[1]
    piece = size // (2 * PLANE * LINE)
    tile = 256
    side_one = x + core * (y - x)
    side_two = y + core * (x - y)
    step_x = 1 - 2 * x
    step_y = 2 - 4 * y
    pair = (rep, other)
    first_hop = (rep + step_x + core * (step_y - step_x), core)
    second_hop = (rep + step_y + core * (step_x - step_y), core)

    def line_of(k):
        return lax.rem(layer + k, LINE)

    def line_to(k):
        return (line_of(k) * PLANE + lax.rem(rep, PLANE), core)

    def rows_of(h, zz, one, two):
        at = (h * LINE + zz) * PLANE + one * 2 + two
        return pl.ds(pl.multiple_of(at * piece, piece), piece)

    barrier = pltpu.get_barrier_semaphore()
    partners = [pair, first_hop, second_hop] + [line_to(k) for k in range(1, LINE)]
    for partner in partners:
        pl.semaphore_signal(barrier, inc=1, device_id=partner, device_id_type=MESH)

    steps = [(h, k) for h in (0, 1) for k in ORDER]
    loads = {}
    for h, k in steps:
        far = pltpu.make_async_copy(parts.at[other, h, line_of(k)], far_part.at[h, k], load_sem.at[0, h, k])
        far.start()
        near = pltpu.make_async_copy(parts.at[core, h, line_of(k)], near_part.at[h, k], load_sem.at[1, h, k])
        near.start()
        loads[h, k] = (far, near)
    mine = pl.ds(pl.multiple_of(core * height, height), height)
    theirs = pl.ds(pl.multiple_of(other * height, height), height)
    pl.semaphore_wait(barrier, len(partners))

    sent = []

    def send(source, target, sems, partner):
        copy = pltpu.make_async_remote_copy(
            src_ref=source, dst_ref=target, send_sem=sems.at[0], recv_sem=sems.at[1],
            device_id=partner, device_id_type=MESH,
        )
        copy.start()
        sent.append(copy)
        return copy

    pairs = {}
    for h, k in steps:
        loads[h, k][0].wait()
        pair_send[h, k] = far_part[h, k].astype(BF16)
        pairs[h, k] = send(pair_send.at[h, k], pair_recv.at[h, k], pair_sem.at[h, k], pair)

    moved = ((stat_in, stat), (basis_in, basis), (first_in, first), (second_in, second), (weights_in, weights))
    keeps = []
    for at, (source, target) in enumerate(moved):
        keep = pltpu.make_async_copy(source.at[core], target.at[mine], keep_sem.at[at])
        keep.start()
        keeps.append(keep)

    for at, (source, target) in enumerate(((stat_right_in, stat_right), (right_in, right))):
        keep = pltpu.make_async_copy(source, target, keep_sem.at[len(moved) + at])
        keep.start()
        keeps.append(keep)

    ones = {}

    def relay_one(h, k):
        loads[h, k][1].wait()
        pairs[h, k].wait_recv()
        near_part[h, k] = near_part[h, k] + pair_recv[h, k].astype(F32)
        one_send[h, k] = near_part[h, k, 1 - side_one].astype(BF16)
        ones[h, k] = send(one_send.at[h, k], one_recv.at[h, k], one_sem.at[h, k], first_hop)

    swaps = []

    def swap_in():
        for at, (source, target) in enumerate(moved):
            swaps.append(send(source.at[other], target.at[mine], swap_sem.at[at], pair))

    twos = {}

    def relay_two(h, k):
        ones[h, k].wait_recv()
        away = 1 - side_two
        two_send[h, k] = (near_part[h, k, side_one, away] + one_recv[h, k, away].astype(F32)).astype(BF16)
        twos[h, k] = send(two_send.at[h, k], two_recv.at[h, k], two_sem.at[h, k], second_hop)

    lines = {}

    def plane_sum(h, k):
        twos[h, k].wait_recv()
        total = near_part[h, k, side_one, side_two] + one_recv[h, k, side_two].astype(F32)
        return total + two_recv[h, k].astype(F32)

    def relay_line(h, k):
        line_send[h, k - 1] = plane_sum(h, k).astype(BF16)
        lines[h, k] = send(line_send.at[h, k - 1], line_recv.at[h, k - 1], line_sem.at[h, k - 1], line_to(k))

    def share(rows, sems, partner):
        return send(grad.at[rows], grad.at[rows], sems, partner)

    glines, gtwos, gones = {}, {}, {}

    def spread(h, k):
        rows = rows_of(h, lax.rem(layer + LINE - k, LINE), side_one, side_two)
        if k:
            glines[h, k].wait_recv()
        gtwos[h, k] = share(rows, gtwo_sem.at[h, k], second_hop)
        gones[h, k, 0] = share(rows, gone_sem.at[h, k, 0], first_hop)

    def forward(h, k):
        gtwos[h, k].wait_recv()
        rows = rows_of(h, lax.rem(layer + LINE - k, LINE), side_one, 1 - side_two)
        gones[h, k, 1] = share(rows, gone_sem.at[h, k, 1], first_hop)

    def finish_own(h):
        total = plane_sum(h, 0)
        for k in range(1, LINE):
            lines[h, k].wait_recv()
            total = total + line_recv[h, k - 1].astype(F32)
        own = rows_of(h, layer, side_one, side_two)
        grad[own, :] = (total * (1.0 / (PLANE * LINE))).astype(BF16)
        for k in GATHER:
            glines[h, k] = share(own, gline_sem.at[h, k - 1], line_to(k))
        spread(h, 0)

    part = size // (2 * LINE)

    def absorb(h, ks, fresh=False):
        groups = []
        for k in ks:
            for way in (0, 1):
                gones[h, k, way].wait_recv()
            groups.append(tile_rows(h * LINE + lax.rem(layer + LINE - k, LINE), part))
        both = jnp.concatenate([grad[group, :] for group in groups], 0)
        added = dot(both, both, ((0,), (0,)))
        rterm[...] = added if fresh else rterm[...] + added

        @pl.loop(0, size // tile)
        def _(at):
            rows = tile_rows(at, tile)
            both_basis = jnp.concatenate([basis[group, rows] for group in groups], 0)
            both = jnp.concatenate([grad[group, :] for group in groups], 0)
            added = dot(both_basis, both, ((0,), (0,)))
            rot_sum[rows, :] = added if fresh else rot_sum[rows, :] + added

    def power_part(at):
        rows = pl.ds(at * (size // LINE), size // LINE)
        power[rows, :] = stat_beta * dot(stat[rows, :].astype(BF16), basis[...])

    relay_one(0, 2)
    relay_one(0, 1)
    relay_one(1, 2)
    relay_two(0, 2)
    relay_one(0, 3)
    swap_in()
    relay_one(1, 3)
    relay_two(1, 2)
    relay_one(1, 1)
    relay_two(0, 1)
    relay_line(0, 2)
    relay_two(0, 3)
    for step in (0, 1):
        swaps[step].wait_recv()
        keeps[step].wait()
    power_part(0)
    relay_one(0, 0)
    relay_line(1, 2)
    relay_two(1, 3)
    relay_two(1, 1)
    relay_line(0, 1)
    relay_one(1, 0)
    relay_line(0, 3)
    relay_two(0, 0)
    relay_line(1, 3)
    relay_line(1, 1)
    relay_two(1, 0)
    finish_own(0)
    power_part(1)
    finish_own(1)
    forward(0, 0)
    spread(0, 2)
    spread(0, 1)
    spread(0, 3)
    forward(0, 2)
    forward(0, 1)
    spread(1, 2)
    spread(1, 3)
    spread(1, 1)
    power_part(2)
    forward(0, 3)
    forward(1, 2)
    forward(1, 3)
    forward(1, 0)
    absorb(0, (0, 1), True)
    forward(1, 1)
    power_part(3)
    absorb(0, (3, 2))
    absorb(1, (3, 2))
    absorb(1, (0, 1))
    swap_right = send(rterm, rterm_far, rterm_sem, pair)
    for step in (2, 3, 4):
        swaps[step].wait_recv()
        keeps[step].wait()
    for keep in keeps[5:]:
        keep.wait()

    tiles = [slice(at, at + tile) for at in range(0, size, tile)]
    for rows in tiles:
        rot[rows, :] = rot_sum[rows, :].astype(BF16)
    squares = None
    for rows in tiles:
        rotated = dot(rot[rows, :], right[...])
        moment = moment_decay * first[rows, :] + (1.0 - moment_decay) * rotated
        square = square_decay * second[rows, :] + (1.0 - square_decay) * rotated * rotated
        first[rows, :] = moment
        second[rows, :] = square
        direction = moment / (jnp.sqrt(square) + epsilon)
        half[rows, :] = dot(direction.astype(BF16), right[...], ((1,), (1,))).astype(BF16)
        value = power[rows, :] + (1.0 - stat_beta) * dot(grad[rows, :], rot[...], ((1,), (1,)))
        power[rows, :] = value
        added = jnp.sum(value * value, axis=0, keepdims=True)
        squares = added if squares is None else squares + added
    scale = lax.rsqrt(jnp.sum(squares) + norm_epsilon)
    for rows in tiles:
        update = dot(basis[rows, :], half[...])
        weights[rows, :] = (weights[rows, :].astype(F32) - learn_rate * update).astype(BF16)
        start[rows, :] = (power[rows, :] * scale).astype(BF16)

    gives = []
    stores = []

    def store(source, target):
        copy = pltpu.make_async_copy(source, target, store_sem.at[len(stores)])
        copy.start()
        stores.append(copy)

    def give(source, target):
        gives.append(send(source, target, give_sem.at[len(gives)], pair))

    give(weights, weights_out.at[core])
    give(first.at[theirs], first_out.at[core])
    give(second.at[theirs], second_out.at[core])
    store(weights, weights_out.at[core])
    store(first.at[mine], first_out.at[core])
    store(second.at[mine], second_out.at[core])

    def emit(sweep_rows):
        spare[theirs, :] = sweep_rows(theirs)
        give(spare.at[theirs], basis_out.at[core])
        basis_out[core] = sweep_rows(mine)

    swap_right.wait_recv()
    width = right.shape[0]

    def right_tile(at, squares):
        rows = tile_rows(at, tile)
        mixed = stat_beta * stat_right[rows, :] + (1.0 - stat_beta) * (rterm[rows, :] + rterm_far[rows, :])
        value = dot(mixed.astype(BF16), right[...])
        rpower[rows, :] = value
        return squares + jnp.sum(value * value)

    rsquares = lax.fori_loop(0, width // tile, right_tile, jnp.float32(0.0))
    rscale = lax.rsqrt(rsquares + norm_epsilon)
    right_out[...] = (rpower[...] * rscale).astype(BF16)

    schulz_mirrored(start, gram, poly, spare, size, tile, emit)

    for copy in gives:
        copy.wait_recv()
    for copy in sent:
        copy.wait_send()
    for copy in stores:
        copy.wait()


def finish_kernel(
    start, weights, basis, first, second, right_out, weights_out, basis_out, first_out, second_out,
    now, spare, gram, store_sem,
):
    moves = ((weights, weights_out), (basis, basis_out), (first, first_out), (second, second_out))
    stores = []
    for at, (source, target) in enumerate(moves):
        store = pltpu.make_async_copy(source, target, store_sem.at[at])
        store.start()
        stores.append(store)
    now[...] = start[...]
    right_out[...] = schulz_sweeps(now, gram, spare, now.shape[0], now.shape[0])[...]
    for store in stores:
        store.wait()


def finish_right(start, *held):
    anywhere = pl.BlockSpec(memory_space=pl.ANY)
    in_vmem = pl.BlockSpec(memory_space=pltpu.VMEM)
    width = start.shape[0]
    return pl.pallas_call(
        finish_kernel,
        out_shape=[jax.ShapeDtypeStruct(a.shape, a.dtype) for a in (start,) + held],
        in_specs=[in_vmem] * 5,
        out_specs=[in_vmem] + [anywhere] * 4,
        scratch_shapes=[pltpu.VMEM((width, width), BF16)] * 3 + [pltpu.SemaphoreType.DMA((4,))],
        compiler_params=pltpu.CompilerParams(vmem_limit_bytes=8 << 20),
    )(start, *held)


def on_device_blocks(
    grad_parts, weights, stat_left, stat_right, basis_left, basis_right, moment_first, moment_second
):
    blocks, height, width = weights.shape
    size = blocks * height
    piece = size // (2 * PLANE * LINE)
    parts = grad_parts.reshape(blocks, 2, LINE, 2, 2, piece, width)
    anywhere = pl.BlockSpec(memory_space=pl.ANY)
    in_vmem = pl.BlockSpec(memory_space=pltpu.VMEM)
    dma = pltpu.SemaphoreType.DMA
    weights_new, left_new, right_start, first_new, second_new = pl.pallas_call(
        step_kernel,
        out_shape=(
            pltpu.VMEM((blocks, size, width), BF16),
            pltpu.VMEM((blocks, height, size), BF16),
            pltpu.VMEM((width, width), BF16),
            pltpu.VMEM((blocks, height, width), F32),
            pltpu.VMEM((blocks, height, width), F32),
        ),
        in_specs=[anywhere] * 8,
        out_specs=(in_vmem,) * 5,
        scratch_shapes=[
            pltpu.VMEM((2, LINE, 2, 2, piece, width), F32),
            pltpu.VMEM((2, LINE, 2, 2, piece, width), F32),
            pltpu.VMEM((2, LINE, 2, 2, piece, width), BF16),
            pltpu.VMEM((2, LINE, 2, 2, piece, width), BF16),
            pltpu.VMEM((2, LINE, 2, piece, width), BF16),
            pltpu.VMEM((2, LINE, 2, piece, width), BF16),
            pltpu.VMEM((2, LINE, piece, width), BF16),
            pltpu.VMEM((2, LINE, piece, width), BF16),
            pltpu.VMEM((2, LINE - 1, piece, width), BF16),
            pltpu.VMEM((2, LINE - 1, piece, width), BF16),
            pltpu.VMEM((size, width), BF16),
            pltpu.VMEM((size, size), BF16),
            pltpu.VMEM((size, size), F32),
            pltpu.VMEM((size, width), F32),
            pltpu.VMEM((size, width), F32),
            pltpu.VMEM((size, width), BF16),
            pltpu.VMEM((size, size), F32),
            pltpu.VMEM((size, width), BF16),
            pltpu.VMEM((size, width), F32),
            pltpu.VMEM((size, width), BF16),
            pltpu.VMEM((size, size), BF16),
            pltpu.VMEM((size, size), BF16),
            pltpu.VMEM((size, size), BF16),
            pltpu.VMEM((size, size), BF16),
            pltpu.VMEM((width, width), F32),
            pltpu.VMEM((width, width), F32),
            pltpu.VMEM((width, width), F32),
            pltpu.VMEM((width, width), F32),
            pltpu.VMEM((width, width), BF16),
            dma((2, 2, LINE)),
            dma((2, LINE, 2)),
            dma((2, LINE, 2)),
            dma((2, LINE, 2)),
            dma((2, LINE - 1, 2)),
            dma((2, LINE - 1, 2)),
            dma((2, LINE, 2)),
            dma((2, LINE, 2, 2)),
            dma((2,)),
            dma((5, 2)),
            dma((7,)),
            dma((4, 2)),
            dma((4,)),
        ],
        compiler_params=pltpu.CompilerParams(
            collective_id=0, has_side_effects=True, vmem_limit_bytes=48 << 20
        ),
    )(parts, weights, stat_left, stat_right, basis_left, basis_right, moment_first, moment_second)
    right_new, weights_new, left_new, first_new, second_new = finish_right(
        right_start, weights_new, left_new, first_new, second_new
    )
    return weights_new, left_new, right_new, first_new, second_new


def solution(mesh):
    fits = mesh.shape["shard"] == 2 and mesh.shape["rep"] == 16
    body = on_device_blocks if fits else on_device
    placed = (
        P("rep", "shard", None, None, None),
        P(None, "shard", None),
        P(None, "shard", None),
        P(),
        P(None, "shard", None),
        P(),
        P(None, "shard", None),
        P(None, "shard", None),
    )
    return jax.shard_map(
        body,
        mesh=mesh,
        in_specs=placed,
        out_specs=(
            P(),
            P(None, "shard", None),
            P(),
            P(None, "shard", None),
            P(None, "shard", None),
        ),
        check_vma=False,
    )
```

```python
import functools

import jax
import jax.numpy as jnp
from jax import lax
from jax.experimental import pallas as pl
from jax.experimental.pallas import tpu as pltpu
from jax.sharding import PartitionSpec as P

NS_ITERS = 3


stat_beta = 0.9
moment_decay = 0.9
square_decay = 0.95
learn_rate = 0.1
epsilon = 1e-08
norm_epsilon = 1e-06
schulz_linear = 3.4445
schulz_cubic = -4.775
schulz_quintic = 2.0315


def schulz_whole(matrix):
    current = matrix
    for sweep_index in range(NS_ITERS):
        gram_matrix = lax.optimization_barrier(
            jnp.dot(current, current.T, preferred_element_type=jnp.float32).astype(jnp.bfloat16)
        )
        poly_matrix = (
            schulz_cubic * gram_matrix.astype(jnp.float32)
            + schulz_quintic * jnp.dot(gram_matrix, gram_matrix, preferred_element_type=jnp.float32)
        ).astype(jnp.bfloat16)
        current = (
            schulz_linear * current.astype(jnp.float32)
            + jnp.dot(poly_matrix, current, preferred_element_type=jnp.float32)
        ).astype(jnp.bfloat16)
    return current


def schulz_split(start_rows):
    current = start_rows
    for sweep_index in range(NS_ITERS):
        gathered = lax.all_gather(current, "shard", axis=1, tiled=True)
        gram_rows = lax.optimization_barrier(
            jnp.einsum(
                "bik,bjk->bij", current, gathered, preferred_element_type=jnp.float32
            ).astype(jnp.bfloat16)
        )
        gram_block = lax.all_gather(gram_rows, "shard", axis=1, tiled=True)
        poly_rows = (
            schulz_cubic * gram_rows.astype(jnp.float32)
            + schulz_quintic
            * jnp.einsum("bij,bjk->bik", gram_rows, gram_block, preferred_element_type=jnp.float32)
        ).astype(jnp.bfloat16)
        current = (
            schulz_linear * current.astype(jnp.float32)
            + jnp.einsum("bij,bjk->bik", poly_rows, gathered, preferred_element_type=jnp.float32)
        ).astype(jnp.bfloat16)
    return current


def on_device(
    grad_parts, weights, stat_left, stat_right, basis_left, basis_right, moment_first, moment_second
):
    block_count = weights.shape[0]
    row_count = weights.shape[1]
    width_kv = weights.shape[2]
    rep_count = lax.axis_size("rep")
    shard_pos = lax.axis_index("shard")
    row_start = shard_pos * row_count
    partial_value = grad_parts[0, 0]
    grad_total = lax.psum(partial_value, ("rep", "shard")) / rep_count
    grad_full = grad_total.astype(jnp.bfloat16)
    grad_rows = lax.dynamic_slice_in_dim(grad_full, row_start, row_count, 1)
    left_new = stat_beta * stat_left + (1.0 - stat_beta) * jnp.einsum(
        "bik,bjk->bij", grad_rows, grad_full, preferred_element_type=jnp.float32
    )
    grad_flat = grad_rows.reshape(block_count * row_count, width_kv)
    right_terms = jnp.dot(grad_flat.T, grad_flat, preferred_element_type=jnp.float32)
    right_new = stat_beta * stat_right + (1.0 - stat_beta) * lax.psum(right_terms, "shard")
    basis_all = lax.all_gather(basis_left, "shard", axis=1, tiled=True)
    power_rows = jnp.einsum(
        "bij,bjk->bik", left_new.astype(jnp.bfloat16), basis_all, preferred_element_type=jnp.float32
    )
    local_squares = jnp.sum(power_rows * power_rows, axis=(1, 2))
    block_squares = lax.psum(local_squares, "shard")
    start_rows = (power_rows * lax.rsqrt(block_squares + norm_epsilon)[:, None, None]).astype(
        jnp.bfloat16
    )
    basis_left_new = schulz_split(start_rows)
    right_power = jnp.dot(
        right_new.astype(jnp.bfloat16), basis_right, preferred_element_type=jnp.float32
    )
    right_start = (
        right_power * lax.rsqrt(jnp.sum(right_power * right_power) + norm_epsilon)
    ).astype(jnp.bfloat16)
    basis_right_new = schulz_whole(right_start)
    local_turn = jnp.einsum(
        "bji,bjk->bik", basis_left, grad_rows, preferred_element_type=jnp.float32
    )
    rot_left = lax.psum_scatter(
        local_turn.astype(jnp.bfloat16), "shard", scatter_dimension=1, tiled=True
    ).astype(jnp.float32)
    rot_flat = rot_left.reshape(block_count * row_count, width_kv).astype(jnp.bfloat16)
    rotated = jnp.dot(rot_flat, basis_right, preferred_element_type=jnp.float32).reshape(
        block_count, row_count, width_kv
    )
    moment_new = moment_decay * moment_first + (1.0 - moment_decay) * rotated
    square_new = square_decay * moment_second + (1.0 - square_decay) * rotated * rotated
    direction = moment_new / (jnp.sqrt(square_new) + epsilon)
    direction_flat = direction.reshape(block_count * row_count, width_kv).astype(jnp.bfloat16)
    half_turn = (
        jnp.dot(direction_flat, basis_right.T, preferred_element_type=jnp.float32)
        .astype(jnp.bfloat16)
        .reshape(block_count, row_count, width_kv)
    )
    half_all = lax.all_gather(half_turn, "shard", axis=1, tiled=True)
    update = jnp.einsum("bij,bjk->bik", basis_left, half_all, preferred_element_type=jnp.float32)
    weight_rows_new = (weights.astype(jnp.float32) - learn_rate * update).astype(jnp.bfloat16)
    weights_new = lax.all_gather(weight_rows_new, "shard", axis=1, tiled=True)
    return (weights_new, basis_left_new, basis_right_new, moment_new, square_new)


MESH = pl.DeviceIdType.MESH
PLANE = 4
LINE = 4
PACKED = 1
CHUNKS = 2
ORDER = (2, 1, 3, 0)
GATHER = (2, 1, 3)
F32 = jnp.float32
BF16 = jnp.bfloat16


def dot(a, b, dims=((1,), (0,))):
    return lax.dot_general(a, b, (dims, ((), ())), preferred_element_type=F32)


def tile_rows(at, tile):
    return pl.ds(pl.multiple_of(at * tile, tile), tile)


def schulz_sweeps(start, gram, spare, size, tile):
    chain = (start, spare, start, spare)
    for sweep in range(NS_ITERS):
        now, later = chain[sweep % 2], chain[sweep % 2 + 1]

        @pl.loop(0, size // tile)
        def _(at):
            rows = tile_rows(at, tile)
            gram[rows, :] = dot(now[rows, :], now[...], ((1,), (1,))).astype(BF16)

        @pl.loop(0, size // tile)
        def _(at):
            rows = tile_rows(at, tile)
            poly = schulz_cubic * gram[rows, :].astype(F32) + schulz_quintic * dot(gram[rows, :], gram[...])
            later[rows, :] = (
                schulz_linear * now[rows, :].astype(F32) + dot(poly.astype(BF16), now[...])
            ).astype(BF16)
    return later


def mirror_product(target, size, tile, product, beside):
    for at in range(0, size, tile):
        low = product(slice(at, size), slice(at, at + tile)).astype(BF16)
        target[at:, at:at + tile] = low
        if at + tile < size:
            target[at:at + tile, at + tile:] = low[tile:].T
        beside(at // tile)


def schulz_mirrored(start, gram, poly, spare, size, tile, scale, beside, emit):
    chain = (start, spare, start)
    for sweep in range(NS_ITERS):
        now = chain[sweep]

        def scaled(value, factor):
            return value * factor if sweep == 0 else value

        mirror_product(
            gram, size, tile,
            lambda rows, cols: scaled(dot(now[rows, :], now[cols, :], ((1,), (1,))), scale * scale),
            lambda strip: beside(2 * sweep, strip),
        )
        mirror_product(
            poly, size, tile,
            lambda rows, cols: schulz_cubic * gram[rows, cols].astype(F32)
            + schulz_quintic * dot(gram[rows, :], gram[:, cols]),
            lambda strip: beside(2 * sweep + 1, strip),
        )

        def sweep_rows(rows):
            value = schulz_linear * now[rows, :].astype(F32) + dot(poly[rows, :], now[...])
            return scaled(value, scale).astype(BF16)

        if sweep + 1 < NS_ITERS:
            chain[sweep + 1][...] = sweep_rows(slice(None))
        else:
            emit(sweep_rows)


def step_kernel(
    parts, weights_in, stat_in, stat_right_in, basis_in, right_in, first_in, second_in,
    weights_out, basis_out, right_out, first_out, second_out,
    far_part, near_part, pair_send, pair_recv, one_send, one_recv, two_send, two_recv, line_send, line_recv,
    grad, basis, stat, first, second, weights,
    power, rot, rot_sum, half, start, spare, gram, poly, rpower, rterm, rterm_far, stat_right, right,
    load_sem, pair_sem, one_sem, two_sem, line_sem, gline_sem, gtwo_sem, gone_sem, rterm_sem, swap_sem, keep_sem,
    give_sem, store_sem,
):
    rep = lax.axis_index("rep")
    core = lax.axis_index("shard")
    other = 1 - core
    layer = rep // PLANE
    y = lax.rem(rep // 2, 2)
    x = lax.rem(rep, 2)
    size = basis.shape[0]
    height = basis_in.shape[1]
    piece = size // (CHUNKS * PLANE * LINE)
    part = size // CHUNKS
    tile = 256
    side_one = x + core * (y - x)
    side_two = y + core * (x - y)
    step_x = 1 - 2 * x
    step_y = 2 - 4 * y
    pair = (rep, other)
    first_hop = (rep + step_x + core * (step_y - step_x), core)
    second_hop = (rep + step_y + core * (step_x - step_y), core)

    def line_of(k):
        return lax.rem(layer + k, LINE)

    def line_to(k):
        return (line_of(k) * PLANE + lax.rem(rep, PLANE), core)

    def rows_of(h, zz, one, two):
        at = (h * LINE + zz) * PLANE + one * 2 + two
        return pl.ds(pl.multiple_of(at * piece, piece), piece)

    barrier = pltpu.get_barrier_semaphore()
    partners = [pair, first_hop, second_hop] + [line_to(k) for k in range(1, LINE)]
    for partner in partners:
        pl.semaphore_signal(barrier, inc=1, device_id=partner, device_id_type=MESH)

    steps = [(h, k) for h in range(CHUNKS) for k in ORDER]
    far_loads, near_loads = {}, {}
    for h, k in steps:
        far_loads[h, k] = pltpu.make_async_copy(
            parts.at[other, h, line_of(k)], far_part.at[h, k], load_sem.at[0, h, k]
        )
        near_loads[h, k] = pltpu.make_async_copy(
            parts.at[core, h, line_of(k)], near_part.at[h, k], load_sem.at[1, h, k]
        )
    for copy in list(far_loads.values()) + list(near_loads.values()):
        copy.start()

    def pack(h, k):
        far_loads[h, k].wait()
        pair_send[h, k] = far_part[h, k].astype(BF16)

    for h, k in steps[:PACKED]:
        pack(h, k)
    mine = pl.ds(pl.multiple_of(core * height, height), height)
    theirs = pl.ds(pl.multiple_of(other * height, height), height)
    pl.semaphore_wait(barrier, len(partners))

    sent = []
    tiles = [slice(at, at + tile) for at in range(0, size, tile)]

    def send(source, target, sems, partner):
        copy = pltpu.make_async_remote_copy(
            src_ref=source, dst_ref=target, send_sem=sems.at[0], recv_sem=sems.at[1],
            device_id=partner, device_id_type=MESH,
        )
        copy.start()
        sent.append(copy)
        return copy

    pairs = {}
    for at, (h, k) in enumerate(steps):
        if at >= PACKED:
            pack(h, k)
        pairs[h, k] = send(pair_send.at[h, k], pair_recv.at[h, k], pair_sem.at[h, k], pair)

    moved = ((stat_in, stat), (basis_in, basis), (first_in, first), (second_in, second), (weights_in, weights))
    keeps = []
    for at, (source, target) in enumerate(moved):
        keep = pltpu.make_async_copy(source.at[core], target.at[mine], keep_sem.at[at])
        keep.start()
        keeps.append(keep)

    for at, (source, target) in enumerate(((stat_right_in, stat_right), (right_in, right))):
        keep = pltpu.make_async_copy(source, target, keep_sem.at[len(moved) + at])
        keep.start()
        keeps.append(keep)

    ones = {}

    def relay_one(h, k):
        near_loads[h, k].wait()
        pairs[h, k].wait_recv()
        near_part[h, k] = near_part[h, k] + pair_recv[h, k].astype(F32)
        one_send[h, k] = near_part[h, k, 1 - side_one].astype(BF16)
        ones[h, k] = send(one_send.at[h, k], one_recv.at[h, k], one_sem.at[h, k], first_hop)

    swaps = []

    def swap_in():
        for at, (source, target) in enumerate(moved):
            swaps.append(send(source.at[other], target.at[mine], swap_sem.at[at], pair))

    twos = {}

    def relay_two(h, k):
        ones[h, k].wait_recv()
        away = 1 - side_two
        two_send[h, k] = (near_part[h, k, side_one, away] + one_recv[h, k, away].astype(F32)).astype(BF16)
        twos[h, k] = send(two_send.at[h, k], two_recv.at[h, k], two_sem.at[h, k], second_hop)

    lines = {}

    def plane_sum(h, k):
        twos[h, k].wait_recv()
        total = near_part[h, k, side_one, side_two] + one_recv[h, k, side_two].astype(F32)
        return total + two_recv[h, k].astype(F32)

    def relay_line(h, k):
        line_send[h, k - 1] = plane_sum(h, k).astype(BF16)
        lines[h, k] = send(line_send.at[h, k - 1], line_recv.at[h, k - 1], line_sem.at[h, k - 1], line_to(k))

    def share(rows, sems, partner):
        return send(grad.at[rows], grad.at[rows], sems, partner)

    glines, gtwos, gones = {}, {}, {}

    def spread(h, k):
        rows = rows_of(h, lax.rem(layer + LINE - k, LINE), side_one, side_two)
        if k:
            glines[h, k].wait_recv()
        gtwos[h, k] = share(rows, gtwo_sem.at[h, k], second_hop)
        gones[h, k, 0] = share(rows, gone_sem.at[h, k, 0], first_hop)

    def forward(h, k):
        gtwos[h, k].wait_recv()
        rows = rows_of(h, lax.rem(layer + LINE - k, LINE), side_one, 1 - side_two)
        gones[h, k, 1] = share(rows, gone_sem.at[h, k, 1], first_hop)

    def finish_own(h):
        total = plane_sum(h, 0)
        for k in range(1, LINE):
            lines[h, k].wait_recv()
            total = total + line_recv[h, k - 1].astype(F32)
        own = rows_of(h, layer, side_one, side_two)
        grad[own, :] = (total * (1.0 / (PLANE * LINE))).astype(BF16)
        for k in GATHER:
            glines[h, k] = share(own, gline_sem.at[h, k - 1], line_to(k))
        spread(h, 0)

    def absorb(h):
        for k in range(LINE):
            for way in (0, 1):
                gones[h, k, way].wait_recv()
        group = slice(h * part, (h + 1) * part)
        for rows in tiles:
            added = dot(basis[group, rows], grad[group, :], ((0,), (0,)))
            if h + 1 < CHUNKS:
                rot_sum[rows, :] = added if h == 0 else rot_sum[rows, :] + added
            else:
                rot[rows, :] = (rot_sum[rows, :] + added).astype(BF16)
        added = dot(grad[group, :], grad[group, :], ((0,), (0,)))
        rterm[...] = added if h == 0 else rterm[...] + added

    def power_part(at):
        rows = pl.ds(at * (size // LINE), size // LINE)
        power[rows, :] = stat_beta * dot(stat[rows, :].astype(BF16), basis[...])

    relay_one(0, 2)
    relay_one(0, 1)
    relay_one(0, 3)
    relay_one(1, 2)
    swap_in()
    relay_two(0, 2)
    relay_one(1, 3)
    relay_two(0, 1)
    relay_two(0, 3)
    relay_one(1, 1)
    relay_one(0, 0)
    relay_two(1, 2)
    relay_one(1, 0)
    relay_line(0, 2)
    relay_two(1, 3)
    relay_line(0, 1)
    relay_two(1, 1)
    relay_line(0, 3)
    relay_two(0, 0)
    relay_line(1, 2)
    relay_line(1, 3)
    relay_line(1, 1)
    finish_own(0)
    relay_two(1, 0)
    forward(0, 0)
    finish_own(1)
    spread(0, 1)
    spread(0, 3)
    forward(1, 0)
    spread(0, 2)
    spread(1, 2)
    spread(1, 1)
    spread(1, 3)
    forward(0, 2)
    forward(0, 1)
    forward(0, 3)
    forward(1, 2)
    forward(1, 1)
    forward(1, 3)
    for step in (0, 1):
        swaps[step].wait_recv()
        keeps[step].wait()
    power_part(0)
    power_part(1)
    power_part(2)
    power_part(3)
    absorb(0)
    absorb(1)
    swap_right = send(rterm, rterm_far, rterm_sem, pair)
    for step in (2, 3, 4):
        swaps[step].wait_recv()
        keeps[step].wait()
    for keep in keeps[5:]:
        keep.wait()

    squares = None
    for rows in tiles:
        value = power[rows, :] + (1.0 - stat_beta) * dot(grad[rows, :], rot[...], ((1,), (1,)))
        start[rows, :] = value.astype(BF16)
        added = jnp.sum(value * value, axis=0, keepdims=True)
        squares = added if squares is None else squares + added
    scale = lax.rsqrt(jnp.sum(squares) + norm_epsilon)

    gives = []
    stores = []

    def store(source, target):
        copy = pltpu.make_async_copy(source, target, store_sem.at[len(stores)])
        copy.start()
        stores.append(copy)

    def give(source, target):
        gives.append(send(source, target, give_sem.at[len(gives)], pair))

    def moment_tile(rows):
        rotated = dot(rot[rows, :], right[...])
        moment = moment_decay * first[rows, :] + (1.0 - moment_decay) * rotated
        square = square_decay * second[rows, :] + (1.0 - square_decay) * rotated * rotated
        first[rows, :] = moment
        second[rows, :] = square
        direction = moment / (jnp.sqrt(square) + epsilon)
        half[rows, :] = dot(direction.astype(BF16), right[...], ((1,), (1,))).astype(BF16)

    def update_tile(rows):
        update = dot(basis[rows, :], half[...])
        weights[rows, :] = (weights[rows, :].astype(F32) - learn_rate * update).astype(BF16)

    def right_start():
        swap_right.wait_recv()
        width = right.shape[0]
        squares = None
        for at in range(0, width, tile):
            rows = slice(at, at + tile)
            mixed = stat_beta * stat_right[rows, :] + (1.0 - stat_beta) * (rterm[rows, :] + rterm_far[rows, :])
            value = dot(mixed.astype(BF16), right[...])
            rpower[rows, :] = value
            added = jnp.sum(value * value, axis=0, keepdims=True)
            squares = added if squares is None else squares + added
        right_out[...] = (rpower[...] * lax.rsqrt(jnp.sum(squares) + norm_epsilon)).astype(BF16)

    def beside(product, strip):
        if product == 0:
            moment_tile(tiles[strip])
        elif product == 1:
            update_tile(tiles[strip])
        elif product == 2 and strip == 0:
            give(first.at[theirs], first_out.at[core])
            give(second.at[theirs], second_out.at[core])
            give(weights, weights_out.at[core])
            store(first.at[mine], first_out.at[core])
            store(second.at[mine], second_out.at[core])
            store(weights, weights_out.at[core])
            right_start()

    def emit(sweep_rows):
        spare[theirs, :] = sweep_rows(theirs)
        give(spare.at[theirs], basis_out.at[core])
        basis_out[core] = sweep_rows(mine)

    schulz_mirrored(start, gram, poly, spare, size, tile, scale, beside, emit)

    for copy in gives:
        copy.wait_recv()
    for copy in sent:
        copy.wait_send()
    for copy in stores:
        copy.wait()


def finish_kernel(
    start, weights, basis, first, second, right_out, weights_out, basis_out, first_out, second_out,
    now, spare, gram, store_sem,
):
    moves = ((weights, weights_out), (basis, basis_out), (first, first_out), (second, second_out))
    stores = []
    for at, (source, target) in enumerate(moves):
        store = pltpu.make_async_copy(source, target, store_sem.at[at])
        store.start()
        stores.append(store)
    now[...] = start[...]
    right_out[...] = schulz_sweeps(now, gram, spare, now.shape[0], now.shape[0])[...]
    for store in stores:
        store.wait()


def finish_right(start, *held):
    anywhere = pl.BlockSpec(memory_space=pl.ANY)
    in_vmem = pl.BlockSpec(memory_space=pltpu.VMEM)
    width = start.shape[0]
    return pl.pallas_call(
        finish_kernel,
        out_shape=[jax.ShapeDtypeStruct(a.shape, a.dtype) for a in (start,) + held],
        in_specs=[in_vmem] * 5,
        out_specs=[in_vmem] + [anywhere] * 4,
        scratch_shapes=[pltpu.VMEM((width, width), BF16)] * 3 + [pltpu.SemaphoreType.DMA((4,))],
        compiler_params=pltpu.CompilerParams(vmem_limit_bytes=8 << 20),
    )(start, *held)


def on_device_blocks(
    grad_parts, weights, stat_left, stat_right, basis_left, basis_right, moment_first, moment_second
):
    blocks, height, width = weights.shape
    size = blocks * height
    piece = size // (CHUNKS * PLANE * LINE)
    parts = grad_parts.reshape(blocks, CHUNKS, LINE, 2, 2, piece, width)
    anywhere = pl.BlockSpec(memory_space=pl.ANY)
    in_vmem = pl.BlockSpec(memory_space=pltpu.VMEM)
    dma = pltpu.SemaphoreType.DMA
    weights_new, left_new, right_start, first_new, second_new = pl.pallas_call(
        step_kernel,
        out_shape=(
            pltpu.VMEM((blocks, size, width), BF16),
            pltpu.VMEM((blocks, height, size), BF16),
            pltpu.VMEM((width, width), BF16),
            pltpu.VMEM((blocks, height, width), F32),
            pltpu.VMEM((blocks, height, width), F32),
        ),
        in_specs=[anywhere] * 8,
        out_specs=(in_vmem,) * 5,
        scratch_shapes=[
            pltpu.VMEM((CHUNKS, LINE, 2, 2, piece, width), F32),
            pltpu.VMEM((CHUNKS, LINE, 2, 2, piece, width), F32),
            pltpu.VMEM((CHUNKS, LINE, 2, 2, piece, width), BF16),
            pltpu.VMEM((CHUNKS, LINE, 2, 2, piece, width), BF16),
            pltpu.VMEM((CHUNKS, LINE, 2, piece, width), BF16),
            pltpu.VMEM((CHUNKS, LINE, 2, piece, width), BF16),
            pltpu.VMEM((CHUNKS, LINE, piece, width), BF16),
            pltpu.VMEM((CHUNKS, LINE, piece, width), BF16),
            pltpu.VMEM((CHUNKS, LINE - 1, piece, width), BF16),
            pltpu.VMEM((CHUNKS, LINE - 1, piece, width), BF16),
            pltpu.VMEM((size, width), BF16),
            pltpu.VMEM((size, size), BF16),
            pltpu.VMEM((size, size), F32),
            pltpu.VMEM((size, width), F32),
            pltpu.VMEM((size, width), F32),
            pltpu.VMEM((size, width), BF16),
            pltpu.VMEM((size, size), F32),
            pltpu.VMEM((size, width), BF16),
            pltpu.VMEM((size, width), F32),
            pltpu.VMEM((size, width), BF16),
            pltpu.VMEM((size, size), BF16),
            pltpu.VMEM((size, size), BF16),
            pltpu.VMEM((size, size), BF16),
            pltpu.VMEM((size, size), BF16),
            pltpu.VMEM((width, width), F32),
            pltpu.VMEM((width, width), F32),
            pltpu.VMEM((width, width), F32),
            pltpu.VMEM((width, width), F32),
            pltpu.VMEM((width, width), BF16),
            dma((2, CHUNKS, LINE)),
            dma((CHUNKS, LINE, 2)),
            dma((CHUNKS, LINE, 2)),
            dma((CHUNKS, LINE, 2)),
            dma((CHUNKS, LINE - 1, 2)),
            dma((CHUNKS, LINE - 1, 2)),
            dma((CHUNKS, LINE, 2)),
            dma((CHUNKS, LINE, 2, 2)),
            dma((2,)),
            dma((5, 2)),
            dma((7,)),
            dma((4, 2)),
            dma((4,)),
        ],
        compiler_params=pltpu.CompilerParams(
            collective_id=0, has_side_effects=True, vmem_limit_bytes=48 << 20
        ),
    )(parts, weights, stat_left, stat_right, basis_left, basis_right, moment_first, moment_second)
    right_new, weights_new, left_new, first_new, second_new = finish_right(
        right_start, weights_new, left_new, first_new, second_new
    )
    return weights_new, left_new, right_new, first_new, second_new


def solution(mesh):
    fits = mesh.shape["shard"] == 2 and mesh.shape["rep"] == 16
    body = on_device_blocks if fits else on_device
    placed = (
        P("rep", "shard", None, None, None),
        P(None, "shard", None),
        P(None, "shard", None),
        P(),
        P(None, "shard", None),
        P(),
        P(None, "shard", None),
        P(None, "shard", None),
    )
    return jax.shard_map(
        body,
        mesh=mesh,
        in_specs=placed,
        out_specs=(
            P(),
            P(None, "shard", None),
            P(),
            P(None, "shard", None),
            P(None, "shard", None),
        ),
        check_vma=False,
    )
```

```python
import functools

import jax
import jax.numpy as jnp
from jax import lax
from jax.experimental import pallas as pl
from jax.experimental.pallas import tpu as pltpu
from jax.sharding import PartitionSpec as P

NS_ITERS = 3


stat_beta = 0.9
moment_decay = 0.9
square_decay = 0.95
learn_rate = 0.1
epsilon = 1e-08
norm_epsilon = 1e-06
schulz_linear = 3.4445
schulz_cubic = -4.775
schulz_quintic = 2.0315


def schulz_whole(matrix):
    current = matrix
    for sweep_index in range(NS_ITERS):
        gram_matrix = lax.optimization_barrier(
            jnp.dot(current, current.T, preferred_element_type=jnp.float32).astype(jnp.bfloat16)
        )
        poly_matrix = (
            schulz_cubic * gram_matrix.astype(jnp.float32)
            + schulz_quintic * jnp.dot(gram_matrix, gram_matrix, preferred_element_type=jnp.float32)
        ).astype(jnp.bfloat16)
        current = (
            schulz_linear * current.astype(jnp.float32)
            + jnp.dot(poly_matrix, current, preferred_element_type=jnp.float32)
        ).astype(jnp.bfloat16)
    return current


def schulz_split(start_rows):
    current = start_rows
    for sweep_index in range(NS_ITERS):
        gathered = lax.all_gather(current, "shard", axis=1, tiled=True)
        gram_rows = lax.optimization_barrier(
            jnp.einsum(
                "bik,bjk->bij", current, gathered, preferred_element_type=jnp.float32
            ).astype(jnp.bfloat16)
        )
        gram_block = lax.all_gather(gram_rows, "shard", axis=1, tiled=True)
        poly_rows = (
            schulz_cubic * gram_rows.astype(jnp.float32)
            + schulz_quintic
            * jnp.einsum("bij,bjk->bik", gram_rows, gram_block, preferred_element_type=jnp.float32)
        ).astype(jnp.bfloat16)
        current = (
            schulz_linear * current.astype(jnp.float32)
            + jnp.einsum("bij,bjk->bik", poly_rows, gathered, preferred_element_type=jnp.float32)
        ).astype(jnp.bfloat16)
    return current


def on_device(
    grad_parts, weights, stat_left, stat_right, basis_left, basis_right, moment_first, moment_second
):
    block_count = weights.shape[0]
    row_count = weights.shape[1]
    width_kv = weights.shape[2]
    rep_count = lax.axis_size("rep")
    shard_pos = lax.axis_index("shard")
    row_start = shard_pos * row_count
    partial_value = grad_parts[0, 0]
    grad_total = lax.psum(partial_value, ("rep", "shard")) / rep_count
    grad_full = grad_total.astype(jnp.bfloat16)
    grad_rows = lax.dynamic_slice_in_dim(grad_full, row_start, row_count, 1)
    left_new = stat_beta * stat_left + (1.0 - stat_beta) * jnp.einsum(
        "bik,bjk->bij", grad_rows, grad_full, preferred_element_type=jnp.float32
    )
    grad_flat = grad_rows.reshape(block_count * row_count, width_kv)
    right_terms = jnp.dot(grad_flat.T, grad_flat, preferred_element_type=jnp.float32)
    right_new = stat_beta * stat_right + (1.0 - stat_beta) * lax.psum(right_terms, "shard")
    basis_all = lax.all_gather(basis_left, "shard", axis=1, tiled=True)
    power_rows = jnp.einsum(
        "bij,bjk->bik", left_new.astype(jnp.bfloat16), basis_all, preferred_element_type=jnp.float32
    )
    local_squares = jnp.sum(power_rows * power_rows, axis=(1, 2))
    block_squares = lax.psum(local_squares, "shard")
    start_rows = (power_rows * lax.rsqrt(block_squares + norm_epsilon)[:, None, None]).astype(
        jnp.bfloat16
    )
    basis_left_new = schulz_split(start_rows)
    right_power = jnp.dot(
        right_new.astype(jnp.bfloat16), basis_right, preferred_element_type=jnp.float32
    )
    right_start = (
        right_power * lax.rsqrt(jnp.sum(right_power * right_power) + norm_epsilon)
    ).astype(jnp.bfloat16)
    basis_right_new = schulz_whole(right_start)
    local_turn = jnp.einsum(
        "bji,bjk->bik", basis_left, grad_rows, preferred_element_type=jnp.float32
    )
    rot_left = lax.psum_scatter(
        local_turn.astype(jnp.bfloat16), "shard", scatter_dimension=1, tiled=True
    ).astype(jnp.float32)
    rot_flat = rot_left.reshape(block_count * row_count, width_kv).astype(jnp.bfloat16)
    rotated = jnp.dot(rot_flat, basis_right, preferred_element_type=jnp.float32).reshape(
        block_count, row_count, width_kv
    )
    moment_new = moment_decay * moment_first + (1.0 - moment_decay) * rotated
    square_new = square_decay * moment_second + (1.0 - square_decay) * rotated * rotated
    direction = moment_new / (jnp.sqrt(square_new) + epsilon)
    direction_flat = direction.reshape(block_count * row_count, width_kv).astype(jnp.bfloat16)
    half_turn = (
        jnp.dot(direction_flat, basis_right.T, preferred_element_type=jnp.float32)
        .astype(jnp.bfloat16)
        .reshape(block_count, row_count, width_kv)
    )
    half_all = lax.all_gather(half_turn, "shard", axis=1, tiled=True)
    update = jnp.einsum("bij,bjk->bik", basis_left, half_all, preferred_element_type=jnp.float32)
    weight_rows_new = (weights.astype(jnp.float32) - learn_rate * update).astype(jnp.bfloat16)
    weights_new = lax.all_gather(weight_rows_new, "shard", axis=1, tiled=True)
    return (weights_new, basis_left_new, basis_right_new, moment_new, square_new)


MESH = pl.DeviceIdType.MESH
PLANE = 4
LINE = 4
PACKED = 1
CHUNKS = 2
ORDER = (2, 1, 3, 0)
GATHER = (2, 1, 3)
F32 = jnp.float32
BF16 = jnp.bfloat16


def dot(a, b, dims=((1,), (0,))):
    return lax.dot_general(a, b, (dims, ((), ())), preferred_element_type=F32)


def tile_rows(at, tile):
    return pl.ds(pl.multiple_of(at * tile, tile), tile)


def schulz_sweeps(start, gram, spare, size, tile, sweeps):
    chain = (start, spare, start, spare)
    for sweep in range(sweeps):
        now, later = chain[sweep % 2], chain[sweep % 2 + 1]

        @pl.loop(0, size // tile)
        def _(at):
            rows = tile_rows(at, tile)
            gram[rows, :] = dot(now[rows, :], now[...], ((1,), (1,))).astype(BF16)

        @pl.loop(0, size // tile)
        def _(at):
            rows = tile_rows(at, tile)
            poly = schulz_cubic * gram[rows, :].astype(F32) + schulz_quintic * dot(gram[rows, :], gram[...])
            later[rows, :] = (
                schulz_linear * now[rows, :].astype(F32) + dot(poly.astype(BF16), now[...])
            ).astype(BF16)
    return later


def mirror_product(target, size, tile, product, beside):
    for at in range(0, size, tile):
        low = product(slice(at, size), slice(at, at + tile)).astype(BF16)
        target[at:, at:at + tile] = low
        if at + tile < size:
            target[at:at + tile, at + tile:] = low[tile:].T
        beside(at // tile)


def schulz_mirrored(start, gram, poly, spare, size, tile, scale, beside, emit):
    chain = (start, spare, start)
    for sweep in range(NS_ITERS):
        now = chain[sweep]

        def scaled(value, factor):
            return value * factor if sweep == 0 else value

        mirror_product(
            gram, size, tile,
            lambda rows, cols: scaled(dot(now[rows, :], now[cols, :], ((1,), (1,))), scale * scale),
            lambda strip: beside(2 * sweep, strip),
        )
        mirror_product(
            poly, size, tile,
            lambda rows, cols: schulz_cubic * gram[rows, cols].astype(F32)
            + schulz_quintic * dot(gram[rows, :], gram[:, cols]),
            lambda strip: beside(2 * sweep + 1, strip),
        )

        def sweep_rows(rows):
            value = schulz_linear * now[rows, :].astype(F32) + dot(poly[rows, :], now[...])
            return scaled(value, scale).astype(BF16)

        if sweep + 1 < NS_ITERS:
            chain[sweep + 1][...] = sweep_rows(slice(None))
        else:
            emit(sweep_rows)


def step_kernel(
    parts, weights_in, stat_in, stat_right_in, basis_in, right_in, first_in, second_in,
    weights_out, basis_out, right_out, first_out, second_out,
    far_part, near_part, pair_send, pair_recv, one_send, one_recv, two_send, two_recv, line_send, line_recv,
    grad, basis, stat, first, second, weights,
    power, rot, rot_sum, half, start, spare, gram, poly, rpower, rterm, rterm_far, stat_right, right, rstart, rgram,
    load_sem, pair_sem, one_sem, two_sem, line_sem, gline_sem, gtwo_sem, gone_sem, rterm_sem, swap_sem, keep_sem,
    give_sem, store_sem,
):
    rep = lax.axis_index("rep")
    core = lax.axis_index("shard")
    other = 1 - core
    layer = rep // PLANE
    y = lax.rem(rep // 2, 2)
    x = lax.rem(rep, 2)
    size = basis.shape[0]
    height = basis_in.shape[1]
    piece = size // (CHUNKS * PLANE * LINE)
    part = size // CHUNKS
    tile = 256
    side_one = x + core * (y - x)
    side_two = y + core * (x - y)
    step_x = 1 - 2 * x
    step_y = 2 - 4 * y
    pair = (rep, other)
    first_hop = (rep + step_x + core * (step_y - step_x), core)
    second_hop = (rep + step_y + core * (step_x - step_y), core)

    def line_of(k):
        return lax.rem(layer + k, LINE)

    def line_to(k):
        return (line_of(k) * PLANE + lax.rem(rep, PLANE), core)

    def rows_of(h, zz, one, two):
        at = (h * LINE + zz) * PLANE + one * 2 + two
        return pl.ds(pl.multiple_of(at * piece, piece), piece)

    barrier = pltpu.get_barrier_semaphore()
    partners = [pair, first_hop, second_hop] + [line_to(k) for k in range(1, LINE)]
    for partner in partners:
        pl.semaphore_signal(barrier, inc=1, device_id=partner, device_id_type=MESH)

    steps = [(h, k) for h in range(CHUNKS) for k in ORDER]
    far_loads, near_loads = {}, {}
    for h, k in steps:
        far_loads[h, k] = pltpu.make_async_copy(
            parts.at[other, h, line_of(k)], far_part.at[h, k], load_sem.at[0, h, k]
        )
        near_loads[h, k] = pltpu.make_async_copy(
            parts.at[core, h, line_of(k)], near_part.at[h, k], load_sem.at[1, h, k]
        )
    for copy in list(far_loads.values()) + list(near_loads.values()):
        copy.start()

    def pack(h, k):
        far_loads[h, k].wait()
        pair_send[h, k] = far_part[h, k].astype(BF16)

    for h, k in steps[:PACKED]:
        pack(h, k)
    mine = pl.ds(pl.multiple_of(core * height, height), height)
    theirs = pl.ds(pl.multiple_of(other * height, height), height)
    pl.semaphore_wait(barrier, len(partners))

    sent = []
    tiles = [slice(at, at + tile) for at in range(0, size, tile)]

    def send(source, target, sems, partner):
        copy = pltpu.make_async_remote_copy(
            src_ref=source, dst_ref=target, send_sem=sems.at[0], recv_sem=sems.at[1],
            device_id=partner, device_id_type=MESH,
        )
        copy.start()
        sent.append(copy)
        return copy

    pairs = {}
    for at, (h, k) in enumerate(steps):
        if at >= PACKED:
            pack(h, k)
        pairs[h, k] = send(pair_send.at[h, k], pair_recv.at[h, k], pair_sem.at[h, k], pair)

    moved = ((stat_in, stat), (basis_in, basis), (first_in, first), (second_in, second), (weights_in, weights))
    keeps = []
    for at, (source, target) in enumerate(moved):
        keep = pltpu.make_async_copy(source.at[core], target.at[mine], keep_sem.at[at])
        keep.start()
        keeps.append(keep)

    for at, (source, target) in enumerate(((stat_right_in, stat_right), (right_in, right))):
        keep = pltpu.make_async_copy(source, target, keep_sem.at[len(moved) + at])
        keep.start()
        keeps.append(keep)

    ones = {}

    def relay_one(h, k):
        near_loads[h, k].wait()
        pairs[h, k].wait_recv()
        near_part[h, k] = near_part[h, k] + pair_recv[h, k].astype(F32)
        one_send[h, k] = near_part[h, k, 1 - side_one].astype(BF16)
        ones[h, k] = send(one_send.at[h, k], one_recv.at[h, k], one_sem.at[h, k], first_hop)

    swaps = []

    def swap_in():
        for at, (source, target) in enumerate(moved):
            swaps.append(send(source.at[other], target.at[mine], swap_sem.at[at], pair))

    twos = {}

    def relay_two(h, k):
        ones[h, k].wait_recv()
        away = 1 - side_two
        two_send[h, k] = (near_part[h, k, side_one, away] + one_recv[h, k, away].astype(F32)).astype(BF16)
        twos[h, k] = send(two_send.at[h, k], two_recv.at[h, k], two_sem.at[h, k], second_hop)

    lines = {}

    def plane_sum(h, k):
        twos[h, k].wait_recv()
        total = near_part[h, k, side_one, side_two] + one_recv[h, k, side_two].astype(F32)
        return total + two_recv[h, k].astype(F32)

    def relay_line(h, k):
        line_send[h, k - 1] = plane_sum(h, k).astype(BF16)
        lines[h, k] = send(line_send.at[h, k - 1], line_recv.at[h, k - 1], line_sem.at[h, k - 1], line_to(k))

    def share(rows, sems, partner):
        return send(grad.at[rows], grad.at[rows], sems, partner)

    glines, gtwos, gones = {}, {}, {}

    def spread(h, k):
        rows = rows_of(h, lax.rem(layer + LINE - k, LINE), side_one, side_two)
        if k:
            glines[h, k].wait_recv()
        gtwos[h, k] = share(rows, gtwo_sem.at[h, k], second_hop)
        gones[h, k, 0] = share(rows, gone_sem.at[h, k, 0], first_hop)

    def forward(h, k):
        gtwos[h, k].wait_recv()
        rows = rows_of(h, lax.rem(layer + LINE - k, LINE), side_one, 1 - side_two)
        gones[h, k, 1] = share(rows, gone_sem.at[h, k, 1], first_hop)

    def finish_own(h):
        total = plane_sum(h, 0)
        for k in range(1, LINE):
            lines[h, k].wait_recv()
            total = total + line_recv[h, k - 1].astype(F32)
        own = rows_of(h, layer, side_one, side_two)
        grad[own, :] = (total * (1.0 / (PLANE * LINE))).astype(BF16)
        for k in GATHER:
            glines[h, k] = share(own, gline_sem.at[h, k - 1], line_to(k))
        spread(h, 0)

    def absorb(h):
        for k in range(LINE):
            for way in (0, 1):
                gones[h, k, way].wait_recv()
        group = slice(h * part, (h + 1) * part)
        for rows in tiles:
            added = dot(basis[group, rows], grad[group, :], ((0,), (0,)))
            if h + 1 < CHUNKS:
                rot_sum[rows, :] = added if h == 0 else rot_sum[rows, :] + added
            else:
                rot[rows, :] = (rot_sum[rows, :] + added).astype(BF16)
        added = dot(grad[group, :], grad[group, :], ((0,), (0,)))
        rterm[...] = added if h == 0 else rterm[...] + added

    def power_part(at):
        rows = pl.ds(at * (size // LINE), size // LINE)
        power[rows, :] = stat_beta * dot(stat[rows, :].astype(BF16), basis[...])

    relay_one(0, 2)
    relay_one(0, 1)
    relay_one(0, 3)
    relay_one(1, 2)
    swap_in()
    relay_two(0, 2)
    relay_one(1, 3)
    relay_two(0, 1)
    relay_two(0, 3)
    relay_one(1, 1)
    relay_one(0, 0)
    relay_two(1, 2)
    relay_one(1, 0)
    relay_line(0, 2)
    relay_two(1, 3)
    relay_line(0, 1)
    relay_two(1, 1)
    relay_line(0, 3)
    relay_two(0, 0)
    relay_line(1, 2)
    relay_line(1, 3)
    relay_line(1, 1)
    finish_own(0)
    relay_two(1, 0)
    forward(0, 0)
    finish_own(1)
    spread(0, 1)
    spread(0, 3)
    forward(1, 0)
    spread(0, 2)
    spread(1, 2)
    spread(1, 1)
    spread(1, 3)
    forward(0, 2)
    forward(0, 1)
    forward(0, 3)
    forward(1, 2)
    forward(1, 1)
    forward(1, 3)
    for step in (0, 1):
        swaps[step].wait_recv()
        keeps[step].wait()
    power_part(0)
    power_part(1)
    power_part(2)
    power_part(3)
    absorb(0)
    absorb(1)
    swap_right = send(rterm, rterm_far, rterm_sem, pair)
    for step in (2, 3, 4):
        swaps[step].wait_recv()
        keeps[step].wait()
    for keep in keeps[5:]:
        keep.wait()

    squares = None
    for rows in tiles:
        value = power[rows, :] + (1.0 - stat_beta) * dot(grad[rows, :], rot[...], ((1,), (1,)))
        start[rows, :] = value.astype(BF16)
        added = jnp.sum(value * value, axis=0, keepdims=True)
        squares = added if squares is None else squares + added
    scale = lax.rsqrt(jnp.sum(squares) + norm_epsilon)

    gives = []
    stores = []

    def store(source, target):
        copy = pltpu.make_async_copy(source, target, store_sem.at[len(stores)])
        copy.start()
        stores.append(copy)

    def give(source, target):
        gives.append(send(source, target, give_sem.at[len(gives)], pair))

    def moment_tile(rows):
        rotated = dot(rot[rows, :], right[...])
        moment = moment_decay * first[rows, :] + (1.0 - moment_decay) * rotated
        square = square_decay * second[rows, :] + (1.0 - square_decay) * rotated * rotated
        first[rows, :] = moment
        second[rows, :] = square
        direction = moment / (jnp.sqrt(square) + epsilon)
        half[rows, :] = dot(direction.astype(BF16), right[...], ((1,), (1,))).astype(BF16)

    def update_tile(rows):
        update = dot(basis[rows, :], half[...])
        weights[rows, :] = (weights[rows, :].astype(F32) - learn_rate * update).astype(BF16)

    def right_start():
        swap_right.wait_recv()
        width = right.shape[0]
        squares = None
        for at in range(0, width, tile):
            rows = slice(at, at + tile)
            mixed = stat_beta * stat_right[rows, :] + (1.0 - stat_beta) * (rterm[rows, :] + rterm_far[rows, :])
            value = dot(mixed.astype(BF16), right[...])
            rpower[rows, :] = value
            added = jnp.sum(value * value, axis=0, keepdims=True)
            squares = added if squares is None else squares + added
        rstart[...] = (rpower[...] * lax.rsqrt(jnp.sum(squares) + norm_epsilon)).astype(BF16)

    def beside(product, strip):
        if product == 0:
            moment_tile(tiles[strip])
        elif product == 1:
            update_tile(tiles[strip])
        elif product == 2 and strip == 0:
            give(first.at[theirs], first_out.at[core])
            give(second.at[theirs], second_out.at[core])
            give(weights, weights_out.at[core])
            store(first.at[mine], first_out.at[core])
            store(second.at[mine], second_out.at[core])
            store(weights, weights_out.at[core])
            right_start()

    def emit(sweep_rows):
        spare[theirs, :] = sweep_rows(theirs)
        give(spare.at[theirs], basis_out.at[core])
        basis_out[core] = sweep_rows(mine)

    schulz_mirrored(start, gram, poly, spare, size, tile, scale, beside, emit)
    schulz_sweeps(rstart, rgram, right_out, right.shape[0], right.shape[0], 1)

    for copy in gives:
        copy.wait_recv()
    for copy in sent:
        copy.wait_send()
    for copy in stores:
        copy.wait()


def finish_kernel(
    start, weights, basis, first, second, right_out, weights_out, basis_out, first_out, second_out,
    now, spare, gram, store_sem,
):
    moves = ((weights, weights_out), (basis, basis_out), (first, first_out), (second, second_out))
    stores = []
    for at, (source, target) in enumerate(moves):
        store = pltpu.make_async_copy(source, target, store_sem.at[at])
        store.start()
        stores.append(store)
    now[...] = start[...]
    right_out[...] = schulz_sweeps(now, gram, spare, now.shape[0], now.shape[0], NS_ITERS - 1)[...]
    for store in stores:
        store.wait()


def finish_right(start, *held):
    anywhere = pl.BlockSpec(memory_space=pl.ANY)
    in_vmem = pl.BlockSpec(memory_space=pltpu.VMEM)
    width = start.shape[0]
    return pl.pallas_call(
        finish_kernel,
        out_shape=[jax.ShapeDtypeStruct(a.shape, a.dtype) for a in (start,) + held],
        in_specs=[in_vmem] * 5,
        out_specs=[in_vmem] + [anywhere] * 4,
        scratch_shapes=[pltpu.VMEM((width, width), BF16)] * 3 + [pltpu.SemaphoreType.DMA((4,))],
        compiler_params=pltpu.CompilerParams(vmem_limit_bytes=8 << 20),
    )(start, *held)


def on_device_blocks(
    grad_parts, weights, stat_left, stat_right, basis_left, basis_right, moment_first, moment_second
):
    blocks, height, width = weights.shape
    size = blocks * height
    piece = size // (CHUNKS * PLANE * LINE)
    parts = grad_parts.reshape(blocks, CHUNKS, LINE, 2, 2, piece, width)
    anywhere = pl.BlockSpec(memory_space=pl.ANY)
    in_vmem = pl.BlockSpec(memory_space=pltpu.VMEM)
    dma = pltpu.SemaphoreType.DMA
    weights_new, left_new, right_start, first_new, second_new = pl.pallas_call(
        step_kernel,
        out_shape=(
            pltpu.VMEM((blocks, size, width), BF16),
            pltpu.VMEM((blocks, height, size), BF16),
            pltpu.VMEM((width, width), BF16),
            pltpu.VMEM((blocks, height, width), F32),
            pltpu.VMEM((blocks, height, width), F32),
        ),
        in_specs=[anywhere] * 8,
        out_specs=(in_vmem,) * 5,
        scratch_shapes=[
            pltpu.VMEM((CHUNKS, LINE, 2, 2, piece, width), F32),
            pltpu.VMEM((CHUNKS, LINE, 2, 2, piece, width), F32),
            pltpu.VMEM((CHUNKS, LINE, 2, 2, piece, width), BF16),
            pltpu.VMEM((CHUNKS, LINE, 2, 2, piece, width), BF16),
            pltpu.VMEM((CHUNKS, LINE, 2, piece, width), BF16),
            pltpu.VMEM((CHUNKS, LINE, 2, piece, width), BF16),
            pltpu.VMEM((CHUNKS, LINE, piece, width), BF16),
            pltpu.VMEM((CHUNKS, LINE, piece, width), BF16),
            pltpu.VMEM((CHUNKS, LINE - 1, piece, width), BF16),
            pltpu.VMEM((CHUNKS, LINE - 1, piece, width), BF16),
            pltpu.VMEM((size, width), BF16),
            pltpu.VMEM((size, size), BF16),
            pltpu.VMEM((size, size), F32),
            pltpu.VMEM((size, width), F32),
            pltpu.VMEM((size, width), F32),
            pltpu.VMEM((size, width), BF16),
            pltpu.VMEM((size, size), F32),
            pltpu.VMEM((size, width), BF16),
            pltpu.VMEM((size, width), F32),
            pltpu.VMEM((size, width), BF16),
            pltpu.VMEM((size, size), BF16),
            pltpu.VMEM((size, size), BF16),
            pltpu.VMEM((size, size), BF16),
            pltpu.VMEM((size, size), BF16),
            pltpu.VMEM((width, width), F32),
            pltpu.VMEM((width, width), F32),
            pltpu.VMEM((width, width), F32),
            pltpu.VMEM((width, width), F32),
            pltpu.VMEM((width, width), BF16),
            pltpu.VMEM((width, width), BF16),
            pltpu.VMEM((width, width), BF16),
            dma((2, CHUNKS, LINE)),
            dma((CHUNKS, LINE, 2)),
            dma((CHUNKS, LINE, 2)),
            dma((CHUNKS, LINE, 2)),
            dma((CHUNKS, LINE - 1, 2)),
            dma((CHUNKS, LINE - 1, 2)),
            dma((CHUNKS, LINE, 2)),
            dma((CHUNKS, LINE, 2, 2)),
            dma((2,)),
            dma((5, 2)),
            dma((7,)),
            dma((4, 2)),
            dma((4,)),
        ],
        compiler_params=pltpu.CompilerParams(
            collective_id=0, has_side_effects=True, vmem_limit_bytes=48 << 20
        ),
    )(parts, weights, stat_left, stat_right, basis_left, basis_right, moment_first, moment_second)
    right_new, weights_new, left_new, first_new, second_new = finish_right(
        right_start, weights_new, left_new, first_new, second_new
    )
    return weights_new, left_new, right_new, first_new, second_new


def solution(mesh):
    fits = mesh.shape["shard"] == 2 and mesh.shape["rep"] == 16
    body = on_device_blocks if fits else on_device
    placed = (
        P("rep", "shard", None, None, None),
        P(None, "shard", None),
        P(None, "shard", None),
        P(),
        P(None, "shard", None),
        P(),
        P(None, "shard", None),
        P(None, "shard", None),
    )
    return jax.shard_map(
        body,
        mesh=mesh,
        in_specs=placed,
        out_specs=(
            P(),
            P(None, "shard", None),
            P(),
            P(None, "shard", None),
            P(None, "shard", None),
        ),
        check_vma=False,
    )
```
